32 devices in a mesh: fsdp: 8 (over y, x, core), seq: 4 (over z).
Axes of the slice: x: 2, y: 2, z: 4, core: 2. Of those that a mesh axis runs over, the one named last changes fastest.
Arguments:
- block_input: bfloat16 [8, 1024, 2048], P('fsdp', 'seq'), may hold values from -6 to 6
- doc_starts: int32 [8, 4], P('fsdp'), may hold values from 0 to 1023, as said below
- attn_gain: bfloat16 [2048], P('fsdp'), may hold values from 0.5 to 1.5
- query_key_value_weight: bfloat16 [2048, 2304], P('fsdp'), may hold values from -0.125 to 0.125
- query_gain: bfloat16 [64], replicated, may hold values from 0.5 to 1.5
- key_gain: bfloat16 [64], replicated, may hold values from 0.5 to 1.5
- out_weight: bfloat16 [1536, 2048], P('fsdp'), may hold values from -0.625 to 0.625
- mlp_gain: bfloat16 [2048], P('fsdp'), may hold values from 0.5 to 1.5
- gateup_weight: bfloat16 [2048, 10240], P('fsdp'), may hold values from -0.125 to 0.125
- down_weight: bfloat16 [5120, 2048], P('fsdp'), may hold values from -0.078125 to 0.078125
- cotangent: bfloat16 [8, 1024, 2048], P('fsdp', 'seq'), may hold values from -6 to 6
Outputs:
- block_output: bfloat16 [8, 1024, 2048], P('fsdp', 'seq')
- input_grad: float32 [8, 1024, 2048], P('fsdp', 'seq')
- attn_gain_grad: float32 [2048], P('fsdp')
- qkv_weight_grad: float32 [2048, 2304], P('fsdp')
- query_gain_grad: float32 [64], replicated
- key_gain_grad: float32 [64], replicated
- out_weight_grad: float32 [1536, 2048], P('fsdp')
- mlp_gain_grad: float32 [2048], P('fsdp')
- gateup_weight_grad: float32 [2048, 10240], P('fsdp')
- down_weight_grad: float32 [5120, 2048], P('fsdp')
The draws below stay inside these ranges and needn't reach their ends.
Inputs may be any that keep to these rules, and one draw needn't show every extreme that they name: `doc_starts`: each row holds the first positions of its 4 documents: the first entry is 0 and the entries strictly increase.
All inputs are finite; a program needn't handle non-finite values.
Results may differ from the reference program's by a relative error of at most 0.02.
Values may be sent and summed in bfloat16 or wider, within the bound.
No kernel may reach another device: no remote copies, remote signals or barrier semaphores. Data moves between devices by JAX's collectives and lax.ppermute only.
A program may use at most 320 MiB of HBM per device.

```python
import math
import jax
import jax.numpy as jnp
from jax import lax

MODEL_WIDTH = 2048
QUERY_HEADS = 24
KEY_VALUE_HEADS = 6
HEAD_WIDTH = 64
FF = 5120
STRETCH_TOKENS = 1024
DOCS = 4
STRETCHES = 8


def draw_doc_starts(key, part):
    row_keys = jax.random.split(key, STRETCHES)

    def one_row(row_key):
        picked = jax.random.permutation(row_key, STRETCH_TOKENS - 1)[:DOCS - 1] + 1
        return jnp.concatenate([jnp.zeros((1,), jnp.int32), jnp.sort(picked).astype(jnp.int32)])

    def ending_row(row_key):
        picked = jax.random.permutation(row_key, STRETCH_TOKENS - 2)[:DOCS - 2] + 1
        return jnp.concatenate([jnp.zeros((1,), jnp.int32), jnp.sort(picked).astype(jnp.int32), jnp.full((1,), STRETCH_TOKENS - 1, jnp.int32)])
    first_row = ending_row(row_keys[0])[None, :]
    other_rows = jax.vmap(one_row)(row_keys[1:])
    return jnp.concatenate([first_row, other_rows], axis=0).astype(jnp.int32)


def steps_of(rng, extent, cuts, low, largest):
    def one(dim, blocks):
        heights = jax.random.uniform(jax.random.fold_in(jax.random.fold_in(rng, 6), dim), (blocks,), jnp.float32, low / len(cuts), largest / len(cuts))
        return jnp.repeat(jnp.exp(heights), extent[dim] // blocks).reshape((-1,) + (1,) * (len(extent) - dim - 1))

    loudness = one(*cuts[0])
    for cut in cuts[1:]:
        loudness = loudness * one(*cut)
    return loudness


def bell_draw(own_key, dims, scale, most, pieces=(), kind=jnp.bfloat16):
    entries = scale * jax.random.normal(own_key, dims, jnp.float32)
    if pieces:
        entries = entries * steps_of(own_key, dims, pieces, -0.22, 0.18)
    return jnp.clip(entries, -most, most).astype(kind)


def setup_inputs(seed: int = 0) -> dict:
    streams_of = jax.random.split(jax.random.key(seed), 12)
    return {
        "block_input": bell_draw(streams_of[0], (STRETCHES, STRETCH_TOKENS, MODEL_WIDTH), 1.0, 6.0, ((0, 8), (1, 4))),
        "doc_starts": draw_doc_starts(jax.random.fold_in(streams_of[11], 71), 0),
        "attn_gain": jnp.clip(1.0 + 0.1 * jax.random.normal(streams_of[2], (MODEL_WIDTH,), jnp.float32), 0.5, 1.5).astype(jnp.bfloat16),
        "query_key_value_weight": bell_draw(streams_of[3], (MODEL_WIDTH, (QUERY_HEADS + 2 * KEY_VALUE_HEADS) * HEAD_WIDTH), MODEL_WIDTH ** -0.5, 0.125, ((0, 8),)),
        "query_gain": jnp.clip(1.0 + 0.1 * jax.random.normal(streams_of[4], (HEAD_WIDTH,), jnp.float32), 0.5, 1.5).astype(jnp.bfloat16),
        "key_gain": jnp.clip(1.0 + 0.1 * jax.random.normal(streams_of[5], (HEAD_WIDTH,), jnp.float32), 0.5, 1.5).astype(jnp.bfloat16),
        "out_weight": bell_draw(streams_of[6], (QUERY_HEADS * HEAD_WIDTH, MODEL_WIDTH), (QUERY_HEADS * HEAD_WIDTH // 16) ** -0.5, 0.625, ((0, 8),)),
        "mlp_gain": jnp.clip(1.0 + 0.1 * jax.random.normal(streams_of[7], (MODEL_WIDTH,), jnp.float32), 0.5, 1.5).astype(jnp.bfloat16),
        "gateup_weight": bell_draw(streams_of[8], (MODEL_WIDTH, 2 * FF), MODEL_WIDTH ** -0.5, 0.125, ((0, 8),)),
        "down_weight": bell_draw(streams_of[9], (FF, MODEL_WIDTH), FF ** -0.5, 0.078125, ((0, 8),)),
        "cotangent": bell_draw(streams_of[10], (STRETCHES, STRETCH_TOKENS, MODEL_WIDTH), 1.0, 6.0, ((0, 8), (1, 4))),
    }


EPSILON = 1e-06
NEG_LARGE = -1e+30
HIGHEST = lax.Precision.HIGHEST

@jax.custom_vjp
def low(v):
    return lax.optimization_barrier(v.astype(jnp.bfloat16)).astype(jnp.float32)

@jax.custom_vjp
def low_back(v):
    return v

def low_keep(v):
    return (low(v), None)

def low_pass(kept, grad):
    return (grad,)

def back_keep(v):
    return (v, None)

def back_low(kept, grad):
    return (low(grad),)
low.defvjp(low_keep, low_pass)
low_back.defvjp(back_keep, back_low)

def matmul_high(left, right):
    return jnp.dot(left, right, precision=HIGHEST)

def inverse_rms(values):
    return lax.rsqrt(lax.optimization_barrier(jnp.mean(values * values, axis=-1, keepdims=True)) + EPSILON)

def rotate(values):
    half_size = values.shape[-1] // 2
    return jnp.concatenate([-values[..., half_size:], values[..., :half_size]], axis=-1)

def rope_tables(position):
    half_size = HEAD_WIDTH // 2
    inverse_freq = jnp.exp(jnp.arange(half_size, dtype=jnp.float32) * (-2.0 * math.log(10000.0) / HEAD_WIDTH))
    angle = position.astype(jnp.float32)[:, None] * inverse_freq[None, :]
    cosine = jnp.concatenate([jnp.cos(angle), jnp.cos(angle)], axis=-1)
    sine = jnp.concatenate([jnp.sin(angle), jnp.sin(angle)], axis=-1)
    return (cosine, sine)

def doc_layout(starts_row):
    index = jnp.arange(STRETCH_TOKENS, dtype=jnp.int32)
    before = starts_row[None, :] <= index[:, None]
    document_segment = lax.optimization_barrier(jnp.sum(before.astype(jnp.int32), axis=-1)).astype(jnp.int32)
    begin = lax.optimization_barrier(jnp.max(jnp.where(before, starts_row[None, :], 0), axis=-1)).astype(jnp.int32)
    return (document_segment, (index - begin).astype(jnp.int32))

def attend_entire_span(inputs):
    queries, keys, values, document_segment = inputs
    heads_per_group = QUERY_HEADS // KEY_VALUE_HEADS
    keys_wide = jnp.repeat(keys, heads_per_group, axis=1)
    values_wide = jnp.repeat(values, heads_per_group, axis=1)
    scores = low_back(jnp.einsum('qhd,khd->hqk', queries, keys_wide, precision=HIGHEST) * HEAD_WIDTH ** (-0.5))
    index = jnp.arange(STRETCH_TOKENS, dtype=jnp.int32)
    allowed = (index[None, :] <= index[:, None]) & (document_segment[None, :] == document_segment[:, None])
    scores = jnp.where(allowed[None], scores, NEG_LARGE)
    row_max = lax.optimization_barrier(jnp.max(scores, axis=-1, keepdims=True))
    weights_exp = jnp.exp(scores - row_max)
    probability = weights_exp / lax.optimization_barrier(jnp.sum(weights_exp, axis=-1, keepdims=True))
    return jnp.einsum('hqk,khd->qhd', low(probability), values_wide, precision=HIGHEST)

def layer(params, inputs, document_segment, docpos):
    attn_gain, query_key_value_weight, query_gain, key_gain, out_weight, mlp_gain, gateup_weight, down_weight = params
    span_count = inputs.shape[0]
    tokens = inputs.reshape(-1, MODEL_WIDTH)
    normed_low = low(tokens * inverse_rms(tokens) * attn_gain)
    projection_result = low_back(matmul_high(normed_low, query_key_value_weight))
    query_total_width = QUERY_HEADS * HEAD_WIDTH
    key_value_width = KEY_VALUE_HEADS * HEAD_WIDTH
    query_raw = projection_result[:, :query_total_width].reshape(-1, QUERY_HEADS, HEAD_WIDTH)
    key_unnormalized = projection_result[:, query_total_width:query_total_width + key_value_width].reshape(-1, KEY_VALUE_HEADS, HEAD_WIDTH)
    value_unprojected = projection_result[:, query_total_width + key_value_width:].reshape(-1, KEY_VALUE_HEADS, HEAD_WIDTH)
    query_normed = query_raw * inverse_rms(query_raw) * query_gain
    key_normed = key_unnormalized * inverse_rms(key_unnormalized) * key_gain
    cosine, sine = rope_tables(docpos.reshape(-1))
    cosine = cosine[:, None, :]
    sine = sine[:, None, :]
    query_reduced_precision = low(low_back(query_normed * cosine + rotate(query_normed) * sine))
    key_reduced_precision = low(low_back(key_normed * cosine + rotate(key_normed) * sine))
    value_reduced_precision = low(low_back(value_unprojected))
    attention_result = lax.map(jax.checkpoint(attend_entire_span), (query_reduced_precision.reshape(span_count, STRETCH_TOKENS, QUERY_HEADS, HEAD_WIDTH), key_reduced_precision.reshape(span_count, STRETCH_TOKENS, KEY_VALUE_HEADS, HEAD_WIDTH), value_reduced_precision.reshape(span_count, STRETCH_TOKENS, KEY_VALUE_HEADS, HEAD_WIDTH), document_segment))
    attn_tok = low(low_back(attention_result.reshape(-1, query_total_width)))
    hidden = tokens + low_back(matmul_high(attn_tok, out_weight))
    mlp_low = low(hidden * inverse_rms(hidden) * mlp_gain)
    gate_up = low_back(matmul_high(mlp_low, gateup_weight))
    gate = gate_up[:, :FF]
    upper = gate_up[:, FF:]
    mixed_low = low(gate * jax.nn.sigmoid(gate) * upper)
    return (hidden + matmul_high(mixed_low, down_weight)).reshape(inputs.shape)

def reference(block_input, doc_starts, attn_gain, query_key_value_weight, query_gain, key_gain, out_weight, mlp_gain, gateup_weight, down_weight, cotangent):
    params = tuple((item.astype(jnp.float32) for item in (attn_gain, query_key_value_weight, query_gain, key_gain, out_weight, mlp_gain, gateup_weight, down_weight)))
    group_size = math.gcd(STRETCHES, max(1, 4096 // STRETCH_TOKENS))
    group_count = STRETCHES // group_size
    document_segment, docpos = jax.vmap(doc_layout)(doc_starts)
    inputs = block_input.astype(jnp.float32).reshape(group_count, group_size, STRETCH_TOKENS, MODEL_WIDTH)
    grads_in = cotangent.astype(jnp.float32).reshape(group_count, group_size, STRETCH_TOKENS, MODEL_WIDTH)
    document_segment = document_segment.reshape(group_count, group_size, STRETCH_TOKENS)
    docpos = docpos.reshape(group_count, group_size, STRETCH_TOKENS)

    def step(totals, block):
        block_x, block_seg, block_pos, block_cot = block
        result, pull_back = jax.vjp(lambda weights, values: layer(weights, values, block_seg, block_pos), params, block_x)
        grad_weights, grad_values = pull_back(block_cot)
        totals = jax.tree.map(lambda left, right: left + right, totals, grad_weights)
        return (totals, (result.astype(jnp.bfloat16), grad_values))
    empty_buffer = tuple((jnp.zeros_like(item) for item in params))
    totals, (results, grad_values) = lax.scan(step, empty_buffer, (inputs, document_segment, docpos, grads_in))
    block_output = results.reshape(STRETCHES, STRETCH_TOKENS, MODEL_WIDTH)
    input_grad = grad_values.reshape(STRETCHES, STRETCH_TOKENS, MODEL_WIDTH)
    return (block_output, input_grad, totals[0], totals[1], totals[2], totals[3], totals[4], totals[5], totals[6], totals[7])
```

```python
from functools import partial
import math

import jax
import jax.numpy as jnp
from jax import lax
from jax.experimental import pallas as pl
from jax.experimental.pallas import tpu as pltpu
from jax.sharding import PartitionSpec as P

QUERY_HEADS = 24
KEY_VALUE_HEADS = 6
HEAD_WIDTH = 64
GROUP = QUERY_HEADS // KEY_VALUE_HEADS
QUERY_WIDTH = QUERY_HEADS * HEAD_WIDTH
KEY_WIDTH = KEY_VALUE_HEADS * HEAD_WIDTH
PAIR_WIDTH = 2 * KEY_WIDTH
PROJ_WIDTH = QUERY_WIDTH + PAIR_WIDTH
LANES = 128
PAD_ROWS = 16

EPSILON = 1e-06
NEG_LARGE = -1e30
SCALE = HEAD_WIDTH ** (-0.5)


F32 = jnp.float32
BF16 = jnp.bfloat16


def peer(k):
    return lax.axis_index("fsdp") ^ k if lax.axis_size("fsdp") == 8 else k


def swap(block, distance):
    size = lax.axis_size("fsdp")
    return lax.ppermute(block, "fsdp", [(i, i ^ distance) for i in range(size)])


def gather_blocks(block):
    size = lax.axis_size("fsdp")
    if size == 8:
        half = block.shape[0] // 2
        across = swap(block, 2)
        along = swap(block, 4)
        core = swap(block, 1)
        low = swap(along[:half], 2)
        high = swap(across[half:], 4)
        across_core = swap(across, 1)
        along_core = swap(along, 1)
        low_core = swap(low, 1)
        high_core = swap(high, 1)
        return [
            block,
            core,
            across,
            across_core,
            along,
            along_core,
            jnp.concatenate([low, high], axis=0),
            jnp.concatenate([low_core, high_core], axis=0),
        ]
    held = lax.all_gather(block, "fsdp", axis=0)
    return [held[k] for k in range(size)]


def add_low(left, right):
    return (left.astype(F32) + right.astype(F32)).astype(BF16)


def scatter_sum(blocks):
    size = lax.axis_size("fsdp")
    if size == 8:
        half = blocks[0].shape[0] // 2
        diag = add_low(blocks[6], swap(blocks[7], 1))
        low = swap(diag[:half], 2)
        high = swap(diag[half:], 4)
        across = add_low(blocks[2], swap(blocks[3], 1))
        along = add_low(blocks[4], swap(blocks[5], 1))
        across_low = swap(across[:half], 2)
        along_high = swap(along[half:], 4)
        own = blocks[0].astype(F32) + swap(blocks[1], 1).astype(F32)
        across_high = swap(add_low(across[half:], high), 2)
        along_low = swap(add_low(along[:half], low), 4)
        from_across = jnp.concatenate([across_low, across_high], axis=0)
        from_along = jnp.concatenate([along_low, along_high], axis=0)
        return own + from_across.astype(F32) + from_along.astype(F32)
    held = lax.psum_scatter(jnp.concatenate(blocks), "fsdp", scatter_dimension=0, tiled=True)
    return held.astype(F32)


def exchange(blocks):
    size = lax.axis_size("fsdp")
    if size == 8:
        return [blocks[0]] + [swap(blocks[k], k) for k in range(1, size)]
    held = lax.all_to_all(jnp.stack(blocks), "fsdp", 0, 0)
    return [held[k] for k in range(size)]


def seq_up(value):
    ranks = lax.axis_size("seq")
    return lax.ppermute(value, "seq", [(j, j + 1) for j in range(ranks - 1)])


def seq_down(value):
    ranks = lax.axis_size("seq")
    return lax.ppermute(value, "seq", [(j + 1, j) for j in range(ranks - 1)])


def seq_sum(value):
    ranks = lax.axis_size("seq")
    if ranks != 4:
        return lax.psum(value, "seq")
    rank = lax.axis_index("seq")
    first = add_low(value, lax.ppermute(value, "seq", [(0, 1), (3, 2)]))
    total = add_low(first, lax.ppermute(first, "seq", [(1, 2), (2, 1)]))
    ends = lax.ppermute(total, "seq", [(1, 0), (2, 3)])
    return jnp.where((rank == 1) | (rank == 2), total, ends)


def to_relative_columns(values, size):
    depth = values.shape[1] // size
    return jnp.concatenate(
        [lax.dynamic_slice_in_dim(values, peer(k) * depth, depth, axis=1) for k in range(size)],
        axis=1,
    )


def rows_to_absolute(pieces):
    depth = pieces[0].shape[0]
    whole = jnp.zeros((depth * len(pieces),) + pieces[0].shape[1:], pieces[0].dtype)
    for k, piece in enumerate(pieces):
        whole = lax.dynamic_update_slice_in_dim(whole, piece, peer(k) * depth, axis=0)
    return whole


def lane_index(shape):
    return lax.broadcasted_iota(jnp.int32, shape, 1)


def head_scale(values):
    low = lane_index(values.shape) < HEAD_WIDTH
    squares = values * values
    first = jnp.sum(jnp.where(low, squares, 0.0), axis=-1, keepdims=True)
    second = jnp.sum(jnp.where(low, 0.0, squares), axis=-1, keepdims=True)
    return jnp.where(
        low,
        lax.rsqrt(first * (1.0 / HEAD_WIDTH) + EPSILON),
        lax.rsqrt(second * (1.0 / HEAD_WIDTH) + EPSILON),
    )


def head_mean(values):
    low = lane_index(values.shape) < HEAD_WIDTH
    first = jnp.sum(jnp.where(low, values, 0.0), axis=-1, keepdims=True)
    second = jnp.sum(jnp.where(low, 0.0, values), axis=-1, keepdims=True)
    return jnp.where(low, first, second) * (1.0 / HEAD_WIDTH)


def turn(values):
    half = HEAD_WIDTH // 2
    first = (lane_index(values.shape) % HEAD_WIDTH) < half
    return jnp.where(
        first, -pltpu.roll(values, LANES - half, 1), pltpu.roll(values, half, 1)
    )


def project_kernel(count, depth, xa_ref, cosine_ref, sine_ref, gain_ref, *refs):
    weights, (raw_ref, query_ref, pair_ref) = refs[:count], refs[count:]
    total = jnp.dot(xa_ref[:, :depth], weights[0][:depth, :], preferred_element_type=F32)
    for k in range(1, count):
        total += jnp.dot(
            xa_ref[:, k * depth : (k + 1) * depth],
            weights[k][:depth, :],
            preferred_element_type=F32,
        )
    raw_ref[...] = total
    column = pl.program_id(0)
    tiles = total.shape[1] // LANES

    def positioned(tile, gain):
        part = total[:, tile * LANES : (tile + 1) * LANES]
        normed = part * head_scale(part) * gain
        return (normed * cosine_ref[...] + turn(normed) * sine_ref[...]).astype(BF16)

    @pl.when(column < 2)
    def _():
        for tile in range(tiles):
            query_ref[:, tile * LANES : (tile + 1) * LANES] = positioned(tile, gain_ref[0:1, :])

    @pl.when(column == 2)
    def _():
        for tile in range(tiles // 2):
            pair_ref[:, tile * LANES : (tile + 1) * LANES] = positioned(tile, gain_ref[1:2, :])
        pair_ref[:, KEY_WIDTH:] = total[:, KEY_WIDTH:].astype(BF16)


def project(xa, cosine, sine, gains, weights, depth):
    rows, width = xa.shape
    count = len(weights)
    block = PAIR_WIDTH
    whole = lambda j: (0, 0)
    return pl.pallas_call(
        partial(project_kernel, count, depth),
        grid=(PROJ_WIDTH // block,),
        in_specs=[
            pl.BlockSpec((rows, width), whole),
            pl.BlockSpec((rows, LANES), whole),
            pl.BlockSpec((rows, LANES), whole),
            pl.BlockSpec((8, LANES), whole),
        ]
        + [pl.BlockSpec((w.shape[0], block), lambda j: (0, j)) for w in weights],
        out_specs=[
            pl.BlockSpec((rows, block), lambda j: (0, j)),
            pl.BlockSpec((rows, block), lambda j: (0, jnp.minimum(j, 1))),
            pl.BlockSpec((rows, block), whole),
        ],
        out_shape=[
            jax.ShapeDtypeStruct((rows, PROJ_WIDTH), F32),
            jax.ShapeDtypeStruct((rows, QUERY_WIDTH), BF16),
            jax.ShapeDtypeStruct((rows, PAIR_WIDTH), BF16),
        ],
        compiler_params=pltpu.CompilerParams(vmem_limit_bytes=48 << 20),
        cost_estimate=pl.CostEstimate(
            flops=2 * rows * width * PROJ_WIDTH,
            bytes_accessed=2 * width * PROJ_WIDTH + 10 * rows * PROJ_WIDTH,
            transcendentals=0,
        ),
        name="project",
    )(xa, cosine, sine, gains, *weights)


def unpack_heads(source_ref, target, count, offset, row, scale=None):
    rows = source_ref.shape[0]
    for h in range(count):
        part = source_ref[:, offset + h * HEAD_WIDTH : offset + (h + 1) * HEAD_WIDTH]
        if scale is not None:
            part = part * scale
        target[h, row : row + rows, :] = part


def pack_heads(source, target_ref, count):
    for h in range(0, count, 2):
        target_ref[:, h * HEAD_WIDTH : (h + 2) * HEAD_WIDTH] = jnp.concatenate(
            [source[h], source[h + 1]], axis=-1
        )


def attend_kernel(ranks, rank_ref, begin_ref, query_ref, *refs):
    pairs, out_ref = refs[:ranks], refs[ranks]
    queries, keys, values, outs, bias = refs[ranks + 1 :]
    rows = query_ref.shape[0]
    rank = rank_ref[0]
    unpack_heads(query_ref, queries, QUERY_HEADS, 0, 0, jnp.asarray(SCALE, BF16))
    for r in range(ranks):
        unpack_heads(pairs[r], keys, KEY_VALUE_HEADS, 0, r * rows)
        unpack_heads(pairs[r], values, KEY_VALUE_HEADS, KEY_WIDTH, r * rows)
        key_at = (rank - r) * rows + lax.broadcasted_iota(jnp.int32, (rows, rows), 1)
        query_at = rank * rows + lax.broadcasted_iota(jnp.int32, (rows, rows), 0)
        allowed = (key_at <= query_at) & (key_at >= begin_ref[...])
        bias[:, r * rows : (r + 1) * rows] = jnp.where(allowed, 0.0, NEG_LARGE)

    def one_head(h, carry):
        group = h // GROUP
        scores = (
            lax.dot_general(
                queries[h], keys[group], (((1,), (1,)), ((), ())), preferred_element_type=F32
            )
            + bias[...]
        )
        top = jnp.max(scores, axis=-1, keepdims=True)
        weight = jnp.exp(scores - top)
        total = jnp.sum(weight, axis=-1, keepdims=True)
        probability = (weight * (1.0 / total)).astype(BF16)
        outs[h] = jnp.dot(probability, values[group], preferred_element_type=F32).astype(BF16)
        return carry

    lax.fori_loop(0, QUERY_HEADS, one_head, 0)
    pack_heads(outs, out_ref, QUERY_HEADS)


def attend(rank, begin, query, pairs):
    rows = query.shape[0]
    ranks = len(pairs)
    vmem = pl.BlockSpec(memory_space=pltpu.VMEM)
    elements = QUERY_HEADS * rows * rows * ranks
    return pl.pallas_call(
        partial(attend_kernel, ranks),
        in_specs=[pl.BlockSpec(memory_space=pltpu.SMEM)] + [vmem] * (2 + ranks),
        out_specs=vmem,
        out_shape=jax.ShapeDtypeStruct((rows, QUERY_WIDTH), BF16),
        scratch_shapes=[
            pltpu.VMEM((QUERY_HEADS, rows, HEAD_WIDTH), BF16),
            pltpu.VMEM((KEY_VALUE_HEADS, ranks * rows, HEAD_WIDTH), BF16),
            pltpu.VMEM((KEY_VALUE_HEADS, ranks * rows, HEAD_WIDTH), BF16),
            pltpu.VMEM((QUERY_HEADS, rows, HEAD_WIDTH), BF16),
            pltpu.VMEM((rows, ranks * rows), F32),
        ],
        compiler_params=pltpu.CompilerParams(vmem_limit_bytes=48 << 20),
        cost_estimate=pl.CostEstimate(
            flops=16 * elements * HEAD_WIDTH,
            bytes_accessed=4 * rows * QUERY_WIDTH + 2 * ranks * rows * PAIR_WIDTH,
            transcendentals=elements,
        ),
        name="attend",
    )(rank.reshape(1), begin[:, None], query, *pairs)


def attend_back_kernel(ranks, rank_ref, begin_ref, query_ref, grad_ref, *refs):
    pairs, grad_query_ref, grad_pair_ref = refs[:ranks], refs[ranks], refs[ranks + 1]
    queries, keys, values, grads, grad_queries, grad_keys, grad_values, bias = refs[ranks + 2 :]
    rows = query_ref.shape[0]
    rank = rank_ref[0]
    unpack_heads(query_ref, queries, QUERY_HEADS, 0, 0, jnp.asarray(SCALE, BF16))
    unpack_heads(grad_ref, grads, QUERY_HEADS, 0, 0)
    for r in range(ranks):
        unpack_heads(pairs[r], keys, KEY_VALUE_HEADS, 0, r * rows)
        unpack_heads(pairs[r], values, KEY_VALUE_HEADS, KEY_WIDTH, r * rows)
        key_at = (rank - r) * rows + lax.broadcasted_iota(jnp.int32, (rows, rows), 0)
        query_at = rank * rows + lax.broadcasted_iota(jnp.int32, (rows, rows), 1)
        allowed = (key_at <= query_at) & (key_at >= begin_ref[...])
        bias[r * rows : (r + 1) * rows, :] = jnp.where(allowed, 0.0, NEG_LARGE)
    grad_keys[...] = jnp.zeros_like(grad_keys)
    grad_values[...] = jnp.zeros_like(grad_values)

    def one_head(h, carry):
        group = h // GROUP
        query, grad = queries[h], grads[h]
        scores = (
            lax.dot_general(
                keys[group], query, (((1,), (1,)), ((), ())), preferred_element_type=F32
            )
            + bias[...]
        )
        top = jnp.max(scores, axis=0, keepdims=True)
        weight = jnp.exp(scores - top)
        total = jnp.sum(weight, axis=0, keepdims=True)
        probability = weight * (1.0 / total)
        grad_prob = lax.dot_general(
            values[group], grad, (((1,), (1,)), ((), ())), preferred_element_type=F32
        )
        inner = jnp.sum(probability * grad_prob, axis=0, keepdims=True)
        grad_score = (probability * (grad_prob - inner)).astype(BF16)
        grad_keys[group] += jnp.dot(grad_score, query, preferred_element_type=F32)
        grad_values[group] += jnp.dot(
            probability.astype(BF16), grad, preferred_element_type=F32
        )
        grad_queries[h] = (
            lax.dot_general(
                grad_score, keys[group], (((0,), (0,)), ((), ())), preferred_element_type=F32
            )
            * SCALE
        ).astype(BF16)
        return carry

    lax.fori_loop(0, QUERY_HEADS, one_head, 0)
    pack_heads(grad_queries, grad_query_ref, QUERY_HEADS)
    for r in range(ranks):
        for source, offset in ((grad_keys, 0), (grad_values, KEY_WIDTH)):
            for g in range(0, KEY_VALUE_HEADS, 2):
                at = offset + g * HEAD_WIDTH
                grad_pair_ref[r, :, at : at + 2 * HEAD_WIDTH] = jnp.concatenate(
                    [
                        source[g, r * rows : (r + 1) * rows, :],
                        source[g + 1, r * rows : (r + 1) * rows, :],
                    ],
                    axis=-1,
                )


def attend_back(rank, begin, query, grad, pairs):
    rows = query.shape[0]
    ranks = len(pairs)
    vmem = pl.BlockSpec(memory_space=pltpu.VMEM)
    elements = QUERY_HEADS * rows * rows * ranks
    heads = pltpu.VMEM((QUERY_HEADS, rows, HEAD_WIDTH), BF16)
    return pl.pallas_call(
        partial(attend_back_kernel, ranks),
        in_specs=[pl.BlockSpec(memory_space=pltpu.SMEM)] + [vmem] * (3 + ranks),
        out_specs=[vmem, vmem],
        out_shape=[
            jax.ShapeDtypeStruct((rows, QUERY_WIDTH), BF16),
            jax.ShapeDtypeStruct((ranks, rows, PAIR_WIDTH), F32),
        ],
        scratch_shapes=[
            heads,
            pltpu.VMEM((KEY_VALUE_HEADS, ranks * rows, HEAD_WIDTH), BF16),
            pltpu.VMEM((KEY_VALUE_HEADS, ranks * rows, HEAD_WIDTH), BF16),
            heads,
            heads,
            pltpu.VMEM((KEY_VALUE_HEADS, ranks * rows, HEAD_WIDTH), F32),
            pltpu.VMEM((KEY_VALUE_HEADS, ranks * rows, HEAD_WIDTH), F32),
            pltpu.VMEM((ranks * rows, rows), F32),
        ],
        compiler_params=pltpu.CompilerParams(vmem_limit_bytes=56 << 20),
        cost_estimate=pl.CostEstimate(
            flops=40 * elements * HEAD_WIDTH,
            bytes_accessed=6 * rows * QUERY_WIDTH + 6 * ranks * rows * PAIR_WIDTH,
            transcendentals=elements,
        ),
        name="attend_back",
    )(rank.reshape(1), begin[None, :], query, grad, *pairs)


def unposition_kernel(turned, grad_ref, raw_ref, cosine_ref, sine_ref, gain_ref, out_ref, sum_ref):
    tiles = grad_ref.shape[1] // LANES
    total = jnp.zeros((1, LANES), F32)
    for tile in range(tiles):
        at = slice(tile * LANES, (tile + 1) * LANES)
        if tile >= turned:
            out_ref[:, at] = grad_ref[:, at]
            continue
        grad = grad_ref[:, at].astype(F32)
        raw = raw_ref[:, at]
        scale = head_scale(raw)
        grad = grad * cosine_ref[...] - turn(grad * sine_ref[...])
        total += jnp.sum(grad * raw * scale, axis=0, keepdims=True)
        grad = grad * gain_ref[0:1, :]
        back = scale * (grad - raw * scale * scale * head_mean(grad * raw))
        out_ref[:, at] = back.astype(BF16)
    total = jnp.broadcast_to(total, sum_ref.shape)

    @pl.when(pl.program_id(0) == 0)
    def _():
        sum_ref[...] = total

    @pl.when(pl.program_id(0) > 0)
    def _():
        sum_ref[...] += total


def unposition(grad, raw, cosine, sine, gain, first_block, turned, block):
    rows, width = grad.shape
    whole = lambda j: (0, 0)
    return pl.pallas_call(
        partial(unposition_kernel, turned),
        grid=(width // block,),
        in_specs=[
            pl.BlockSpec((rows, block), lambda j: (0, j)),
            pl.BlockSpec((rows, block), lambda j: (0, first_block + j)),
            pl.BlockSpec((rows, LANES), whole),
            pl.BlockSpec((rows, LANES), whole),
            pl.BlockSpec((8, LANES), whole),
        ],
        out_specs=[
            pl.BlockSpec((rows, block), lambda j: (0, j)),
            pl.BlockSpec((8, LANES), whole),
        ],
        out_shape=[
            jax.ShapeDtypeStruct((rows, width), BF16),
            jax.ShapeDtypeStruct((8, LANES), F32),
        ],
        compiler_params=pltpu.CompilerParams(vmem_limit_bytes=32 << 20),
        cost_estimate=pl.CostEstimate(
            flops=40 * rows * width, bytes_accessed=8 * rows * width, transcendentals=0
        ),
        name="unposition",
    )(grad, raw, cosine, sine, gain)


def inverse_rms(values):
    return lax.rsqrt(jnp.mean(values * values, axis=-1, keepdims=True) + EPSILON)


def norm_back(grad_out, values, scale):
    return scale * (
        grad_out - values * scale * scale * jnp.mean(grad_out * values, axis=-1, keepdims=True)
    )


def rope_tables(position):
    half_size = HEAD_WIDTH // 2
    inverse_freq = jnp.exp(
        jnp.arange(half_size, dtype=F32) * (-2.0 * math.log(10000.0) / HEAD_WIDTH)
    )
    angle = position.astype(F32)[:, None] * inverse_freq[None, :]
    copies = LANES // half_size
    return (jnp.tile(jnp.cos(angle), (1, copies)), jnp.tile(jnp.sin(angle), (1, copies)))


def gain_rows(gain):
    wide = jnp.tile(gain.astype(F32), LANES // HEAD_WIDTH)
    return jnp.broadcast_to(wide[None, :], (8, LANES))


def shards(
    block_input,
    doc_starts,
    attn_gain,
    query_key_value_weight,
    query_gain,
    key_gain,
    out_weight,
    mlp_gain,
    gateup_weight,
    down_weight,
    cotangent,
):
    count, rows, width = block_input.shape
    assert count == 1
    size = lax.axis_size("fsdp")
    ranks = lax.axis_size("seq")
    me = lax.axis_index("fsdp")
    rank = lax.axis_index("seq")
    depth = query_key_value_weight.shape[0]
    hidden_rows = out_weight.shape[0]
    units = down_weight.shape[0]

    gain_pad = jnp.zeros((PAD_ROWS, PROJ_WIDTH), BF16)
    gain_pad = gain_pad.at[0, :depth].set(attn_gain).at[1, :depth].set(mlp_gain)
    qkv_pieces = gather_blocks(jnp.concatenate([query_key_value_weight, gain_pad], axis=0))

    grad_low = cotangent.reshape(rows, width)
    mixed_pieces = gather_blocks(jnp.concatenate([grad_low, out_weight], axis=0))
    grad_all = jnp.concatenate([piece[:rows] for piece in mixed_pieces], axis=0)
    out_all = rows_to_absolute([piece[rows:] for piece in mixed_pieces])

    gateup_split = gateup_weight.reshape(depth, 2, size, units)
    gateup_pieces = exchange(
        [
            lax.dynamic_index_in_dim(gateup_split, peer(k), axis=2, keepdims=False).reshape(
                depth, 2 * units
            )
            for k in range(size)
        ]
    )
    gateup_mine = rows_to_absolute(gateup_pieces)

    position = rank * rows + jnp.arange(rows, dtype=jnp.int32)
    starts = doc_starts.reshape(-1)
    begin = jnp.max(
        jnp.where(starts[None, :] <= position[:, None], starts[None, :], 0), axis=-1
    )
    cosine, sine = rope_tables(position - begin)
    query_gains, key_gains = gain_rows(query_gain), gain_rows(key_gain)

    inputs = to_relative_columns(block_input.reshape(rows, width), size).astype(F32)
    scale_attn = inverse_rms(inputs)
    normed_attn = inputs * scale_attn
    gain_attn = jnp.concatenate([piece[depth, :depth] for piece in qkv_pieces]).astype(F32)
    normed_low = (normed_attn * gain_attn).astype(BF16)
    mix_gains = jnp.concatenate([query_gains[:1], key_gains[:1], query_gains[:6]], axis=0)
    raw, query, pair = project(normed_low, cosine, sine, mix_gains, qkv_pieces, depth)
    pairs = [pair]
    for _ in range(ranks - 1):
        pairs.append(seq_up(pairs[-1]))
    attn_tok = attend(rank, begin, query, pairs)
    own_inputs = block_input.reshape(rows, width).astype(F32)
    hidden = own_inputs + jnp.dot(attn_tok, out_all, preferred_element_type=F32)

    gain_stack = jnp.stack([piece[depth + 1, :depth] for piece in qkv_pieces])
    gain_mlp = gain_stack[peer(jnp.arange(size))].reshape(width).astype(F32)
    scale_mlp = inverse_rms(hidden)
    normed_mlp = hidden * scale_mlp
    mlp_low = (normed_mlp * gain_mlp).astype(BF16)
    mlp_all = jnp.concatenate(gather_blocks(mlp_low), axis=0)
    grad_mixed = lax.dot_general(
        grad_all, down_weight, (((1,), (1,)), ((), ())), preferred_element_type=F32
    )
    gate_up = jnp.dot(mlp_all, gateup_mine, preferred_element_type=F32)
    gate = gate_up[:, :units]
    upper = gate_up[:, units:]
    sigmoid_gate = jax.nn.sigmoid(gate)
    activated = gate * sigmoid_gate
    mixed_low = (activated * upper).astype(BF16)
    grad_gate = grad_mixed * upper * sigmoid_gate * (1.0 + gate * (1.0 - sigmoid_gate))
    grad_upper = grad_mixed * activated
    grad_gu_low = jnp.concatenate([grad_gate, grad_upper], axis=-1).astype(BF16)
    grad_mlp_part = lax.dot_general(
        grad_gu_low, gateup_mine, (((1,), (1,)), ((), ())), preferred_element_type=F32
    ).astype(BF16)
    grad_mlp_in = scatter_sum([grad_mlp_part[k * rows : (k + 1) * rows] for k in range(size)])

    grad_down = lax.dot_general(
        mixed_low, grad_all, (((0,), (0,)), ((), ())), preferred_element_type=F32
    ).astype(BF16)
    chunk = units // 2
    total_down = jnp.concatenate(
        [seq_sum(grad_down[:chunk]), seq_sum(grad_down[chunk:])], axis=0
    ).astype(F32)

    grad_gateup = lax.dot_general(
        mlp_all, grad_gu_low, (((0,), (0,)), ((), ())), preferred_element_type=F32
    ).astype(BF16)
    gateup_back = exchange(
        [
            lax.dynamic_slice_in_dim(grad_gateup, peer(k) * depth, depth, axis=0)
            for k in range(size)
        ]
    )
    total_gateup = jnp.zeros((depth, 2 * units * size), F32)
    step = max(1, size // 4)
    for k in range(0, size, step):
        summed = seq_sum(jnp.concatenate(gateup_back[k : k + step], axis=0)).astype(F32)
        for j in range(step):
            for half in range(2):
                total_gateup = lax.dynamic_update_slice(
                    total_gateup,
                    summed[j * depth : (j + 1) * depth, half * units : (half + 1) * units],
                    (0, (half * size + peer(k + j)) * units),
                )

    out_part = jnp.dot(mixed_low, down_weight, preferred_element_type=F32).astype(BF16)
    result = hidden + scatter_sum([out_part[k * rows : (k + 1) * rows] for k in range(size)])
    block_output = result.astype(BF16).reshape(block_input.shape)

    grad_mlp_gain = jnp.sum(grad_mlp_in * normed_mlp, axis=0)
    grad_hidden = grad_low.astype(F32) + norm_back(grad_mlp_in * gain_mlp, hidden, scale_mlp)
    grad_hidden_low = grad_hidden.astype(BF16)

    grad_attn_low = lax.dot_general(
        grad_hidden_low, out_all, (((1,), (1,)), ((), ())), preferred_element_type=F32
    ).astype(BF16)
    grad_query, grad_pairs = attend_back(rank, begin, query, grad_attn_low, pairs)
    carry = grad_pairs[ranks - 1].astype(BF16)
    for r in range(ranks - 2, -1, -1):
        carry = (grad_pairs[r] + seq_down(carry).astype(F32)).astype(BF16)
    grad_query_raw, query_sum = unposition(
        grad_query, raw, cosine, sine, query_gains, 0, 4, 4 * LANES
    )
    grad_pair_raw, key_sum = unposition(
        carry, raw, cosine, sine, key_gains, QUERY_WIDTH // PAIR_WIDTH, 3, PAIR_WIDTH
    )
    columns = jnp.concatenate(
        exchange([normed_low[:, k * depth : (k + 1) * depth] for k in range(size)]), axis=0
    )
    query_all = jnp.concatenate(gather_blocks(grad_query_raw), axis=0)
    pair_all = jnp.concatenate(gather_blocks(grad_pair_raw), axis=0)
    contract = (((0,), (0,)), ((), ()))
    grad_q_weight = lax.dot_general(
        columns, query_all, contract, preferred_element_type=F32
    ).astype(BF16)
    grad_kv_weight = lax.dot_general(
        columns, pair_all, contract, preferred_element_type=F32
    ).astype(BF16)
    total_qkv = jnp.concatenate(
        [seq_sum(grad_q_weight), seq_sum(grad_kv_weight)], axis=1
    ).astype(F32)

    grad_out = lax.dot_general(
        attn_tok, grad_hidden_low, contract, preferred_element_type=F32
    ).astype(BF16)
    shard_out = scatter_sum(
        [
            lax.dynamic_slice_in_dim(grad_out, peer(k) * hidden_rows, hidden_rows, axis=0)
            for k in range(size)
        ]
    )
    total_out = seq_sum(shard_out.astype(BF16)).astype(F32)

    qkv_all = jnp.concatenate([piece[:depth] for piece in qkv_pieces], axis=0)
    grad_proj = jnp.concatenate([grad_query_raw, grad_pair_raw], axis=1)
    grad_attn_in = lax.dot_general(
        grad_proj, qkv_all, (((1,), (1,)), ((), ())), preferred_element_type=F32
    )
    grad_attn_gain = jnp.sum(grad_attn_in * normed_attn, axis=0)
    back = norm_back(grad_attn_in * gain_attn, inputs, scale_attn)
    input_grad = grad_hidden + to_relative_columns(back, size)

    grad_attn_gain = grad_attn_gain.reshape(size, depth)[peer(jnp.arange(size))].reshape(width)
    small = jnp.concatenate([grad_attn_gain, grad_mlp_gain, query_sum[0], key_sum[0]])
    small = lax.psum(small, ("fsdp", "seq"))
    total_attn_gain = lax.dynamic_slice_in_dim(small, me * depth, depth)
    total_mlp_gain = lax.dynamic_slice_in_dim(small, width + me * depth, depth)
    heads = small[2 * width :].reshape(2, LANES // HEAD_WIDTH, HEAD_WIDTH).sum(axis=1)
    return (
        block_output,
        input_grad.reshape(block_input.shape),
        total_attn_gain,
        total_qkv,
        heads[0],
        heads[1],
        total_out,
        total_mlp_gain,
        total_gateup,
        total_down,
    )


def solution(mesh):
    return jax.shard_map(
        shards,
        mesh=mesh,
        in_specs=(
            P("fsdp", "seq", None),
            P("fsdp", None),
            P("fsdp"),
            P("fsdp", None),
            P(),
            P(),
            P("fsdp", None),
            P("fsdp"),
            P("fsdp", None),
            P("fsdp", None),
            P("fsdp", "seq", None),
        ),
        out_specs=(
            P("fsdp", "seq", None),
            P("fsdp", "seq", None),
            P("fsdp"),
            P("fsdp", None),
            P(),
            P(),
            P("fsdp", None),
            P("fsdp"),
            P("fsdp", None),
            P("fsdp", None),
        ),
        check_vma=False,
    )
```

```python
from functools import partial
import math

import jax
import jax.numpy as jnp
from jax import lax
from jax.experimental import pallas as pl
from jax.experimental.pallas import tpu as pltpu
from jax.sharding import PartitionSpec as P


QUERY_HEADS = 24
KEY_VALUE_HEADS = 6
HEAD_WIDTH = 64
GROUP = QUERY_HEADS // KEY_VALUE_HEADS
QUERY_WIDTH = QUERY_HEADS * HEAD_WIDTH
KEY_WIDTH = KEY_VALUE_HEADS * HEAD_WIDTH
PAIR_WIDTH = 2 * KEY_WIDTH
PROJ_WIDTH = QUERY_WIDTH + PAIR_WIDTH
LANES = 128
FSDP, SEQ = "fsdp", "seq"

EPSILON = 1e-06
NEG_LARGE = -1e30
SCALE = HEAD_WIDTH ** (-0.5)


F32 = jnp.float32
BF16 = jnp.bfloat16


def tuned():
    return lax.axis_size(FSDP) == 8 and lax.axis_size(SEQ) == 4


def peer(k):
    return lax.axis_index(FSDP) ^ k if tuned() else k


def swap(block, distance):
    size = lax.axis_size(FSDP)
    return lax.ppermute(block, FSDP, [(i, i ^ distance) for i in range(size)])


def seq_move(value, pairs):
    return lax.ppermute(value, SEQ, pairs)


def after(values, gate):
    return lax.optimization_barrier((*values, gate))[:-1]


def gather_start(block):
    if not tuned():
        return lax.all_gather(block, FSDP, axis=0)
    return (block, swap(block, 1), swap(block, 2), swap(block, 4))


def gather_finish(held, gate=None):
    if not tuned():
        return [(held[k],) for k in range(held.shape[0])]
    block, core, across, along = held
    if gate is not None:
        across, along = after((across, along), gate)
    half = block.shape[0] // 2
    low = swap(along[:half], 2)
    high = swap(across[half:], 4)
    across_core = swap(across, 1)
    along_core = swap(along, 1)
    low_core = swap(low, 1)
    high_core = swap(high, 1)
    return [
        (block,),
        (core,),
        (across,),
        (across_core,),
        (along,),
        (along_core,),
        (low, high),
        (low_core, high_core),
    ]


def gather_direct(block):
    if not tuned():
        return gather_finish(gather_start(block))
    core = swap(block, 1)
    across = swap(block, 2)
    along = swap(block, 4)
    diagonal = swap(block, 6)
    pieces = [block, core]
    for part in (across, along, diagonal):
        pieces += [part, swap(part, 1)]
    return [(piece,) for piece in pieces]


def joined(entries):
    return [e[0] if len(e) == 1 else jnp.concatenate(e, axis=0) for e in entries]


def laid_out(entries):
    out = []
    for k, entry in enumerate(entries):
        at = 0
        for part in entry:
            out.append((k, at, part))
            at += part.shape[0]
    return out


def gather_small(block):
    if not tuned():
        return lax.all_gather(block, FSDP, axis=0)
    held = block[None]
    for distance in (1, 2, 4):
        held = jnp.concatenate([held, swap(held, distance)], axis=0)
    return held


def add_low(left, right):
    return (left.astype(F32) + right.astype(F32)).astype(BF16)


def scatter_sum(blocks):
    if not tuned():
        held = jnp.concatenate(blocks)
        held = lax.psum_scatter(held, FSDP, scatter_dimension=0, tiled=True)
        return held.astype(F32)
    half = blocks[0].shape[0] // 2
    from_core = [swap(blocks[2 * k + 1], 1) for k in range(4)]
    across = add_low(blocks[2], from_core[1])
    across_low = swap(across[:half], 2)
    along = add_low(blocks[4], from_core[2])
    along_high = swap(along[half:], 4)
    diag = add_low(blocks[6], from_core[3])
    low = swap(diag[:half], 2)
    high = swap(diag[half:], 4)
    across_high = swap(add_low(across[half:], high), 2)
    along_low = swap(add_low(along[:half], low), 4)
    own = blocks[0].astype(F32) + from_core[0].astype(F32)
    from_across = jnp.concatenate([across_low, across_high], axis=0)
    from_along = jnp.concatenate([along_low, along_high], axis=0)
    return own + from_across.astype(F32) + from_along.astype(F32)


def scatter_direct(even, odd):
    came = swap(odd, 1)
    own, across, along, diagonal = (add_low(even[j], came[j]) for j in range(4))
    across = swap(across, 2)
    along = swap(along, 4)
    diagonal = swap(diagonal, 6)
    return own.astype(F32) + across.astype(F32) + along.astype(F32) + diagonal.astype(F32)


def exchange(blocks):
    size = len(blocks)
    if tuned():
        return [blocks[0]] + [swap(blocks[k], k) for k in range(1, size)]
    held = lax.all_to_all(jnp.stack(blocks), FSDP, 0, 0)
    return [held[k] for k in range(size)]


def exchange_tokens(held):
    if not tuned():
        return lax.all_to_all(held, FSDP, 0, 0).reshape(-1, held.shape[2])
    came = None
    for distance in (1, 2, 4):
        if came is not None:
            held = jnp.concatenate([split[:, 0], came], axis=1)
        split = held.reshape((-1, 2) + held.shape[1:])
        leaving = split[:, 1]
        came = swap(leaving, distance)
    return jnp.concatenate([split[:, 0], came], axis=1)[0]


def seq_sum(value, gate=None):
    if not tuned():
        return lax.psum(value, SEQ)
    rank = lax.axis_index(SEQ)
    first = add_low(value, seq_move(value, [(0, 1), (3, 2)]))
    other = seq_move(first, [(1, 2), (2, 1)])
    total = add_low(first, other)
    ends = seq_move(total, [(1, 0), (2, 3)])
    if gate is not None:
        total, ends = after((total, ends), gate)
    return jnp.where((rank == 1) | (rank == 2), total, ends)


def sum_small(values):
    if not tuned():
        return lax.psum(values, (FSDP, SEQ))
    values = values.reshape(-1, LANES)
    for distance in (1, 2, 4):
        came = swap(values, distance)
        values = values + came
    for distance in (1, 2):
        pairs = [(j, j ^ distance) for j in range(4)]
        came = seq_move(values, pairs)
        values = values + came
    return values.reshape(-1)


def rows_to_absolute(pieces):
    depth = pieces[0].shape[0]
    whole = jnp.zeros((depth * len(pieces),) + pieces[0].shape[1:], pieces[0].dtype)
    for k, piece in enumerate(pieces):
        whole = lax.dynamic_update_slice_in_dim(whole, piece, peer(k) * depth, axis=0)
    return whole


def lane_index(shape):
    return lax.broadcasted_iota(jnp.int32, shape, 1)


def head_scale(values):
    low = lane_index(values.shape) < HEAD_WIDTH
    squares = values * values
    first = jnp.sum(jnp.where(low, squares, 0.0), axis=-1, keepdims=True)
    second = jnp.sum(jnp.where(low, 0.0, squares), axis=-1, keepdims=True)
    return jnp.where(
        low,
        lax.rsqrt(first * (1.0 / HEAD_WIDTH) + EPSILON),
        lax.rsqrt(second * (1.0 / HEAD_WIDTH) + EPSILON),
    )


def head_mean(values):
    low = lane_index(values.shape) < HEAD_WIDTH
    first = jnp.sum(jnp.where(low, values, 0.0), axis=-1, keepdims=True)
    second = jnp.sum(jnp.where(low, 0.0, values), axis=-1, keepdims=True)
    return jnp.where(low, first, second) * (1.0 / HEAD_WIDTH)


def turn(values):
    half = HEAD_WIDTH // 2
    first = (lane_index(values.shape) % HEAD_WIDTH) < half
    return jnp.where(
        first, -pltpu.roll(values, LANES - half, 1), pltpu.roll(values, half, 1)
    )


def block_start(k, at, depth, device, relative):
    if not relative:
        return k * depth + at
    return pl.multiple_of((device ^ k) * depth + at, LANES)


def project_kernel(layout, depth, relative, place_ref, xa_ref, cosine_ref, sine_ref, gain_ref, *refs):
    count = len(layout)
    weights, (raw_ref, query_ref, pair_ref, split_ref) = refs[:count], refs[count:]
    device = place_ref[1]
    total = None
    for weight, (k, at, high) in zip(weights, layout):
        left = xa_ref[:, pl.ds(block_start(k, at, depth, device, relative), high)]
        term = jnp.dot(left, weight[...], preferred_element_type=F32)
        total = term if total is None else total + term
        split_ref[k, :, at : at + high] = left
    raw_ref[...] = total
    column = pl.program_id(0)
    tiles = total.shape[1] // LANES

    def positioned(tile, gain):
        part = total[:, tile * LANES : (tile + 1) * LANES]
        normed = part * head_scale(part) * gain
        return (normed * cosine_ref[...] + turn(normed) * sine_ref[...]).astype(BF16)

    @pl.when(column < 2)
    def _():
        for tile in range(tiles):
            query_ref[:, tile * LANES : (tile + 1) * LANES] = positioned(tile, gain_ref[0:1, :])

    @pl.when(column == 2)
    def _():
        for tile in range(tiles // 2):
            pair_ref[:, tile * LANES : (tile + 1) * LANES] = positioned(tile, gain_ref[1:2, :])
        pair_ref[:, KEY_WIDTH:] = total[:, KEY_WIDTH:].astype(BF16)


def project(place, xa, cosine, sine, gains, entries, depth):
    rows, width = xa.shape
    block = PAIR_WIDTH
    parts = laid_out(entries)
    layout = tuple((k, at, part.shape[0]) for k, at, part in parts)
    whole = lambda j: (0, 0)
    return pl.pallas_call(
        partial(project_kernel, layout, depth, tuned()),
        grid=(PROJ_WIDTH // block,),
        in_specs=[
            pl.BlockSpec(memory_space=pltpu.SMEM),
            pl.BlockSpec((rows, width), whole),
            pl.BlockSpec((rows, LANES), whole),
            pl.BlockSpec((rows, LANES), whole),
            pl.BlockSpec((8, LANES), whole),
        ]
        + [pl.BlockSpec((part.shape[0], block), lambda j: (0, j)) for _, _, part in parts],
        out_specs=[
            pl.BlockSpec((rows, block), lambda j: (0, j)),
            pl.BlockSpec((rows, block), lambda j: (0, jnp.minimum(j, 1))),
            pl.BlockSpec((rows, block), whole),
            pl.BlockSpec((len(entries), rows, depth), lambda j: (0, 0, 0)),
        ],
        out_shape=[
            jax.ShapeDtypeStruct((rows, PROJ_WIDTH), F32),
            jax.ShapeDtypeStruct((rows, QUERY_WIDTH), BF16),
            jax.ShapeDtypeStruct((rows, PAIR_WIDTH), BF16),
            jax.ShapeDtypeStruct((len(entries), rows, depth), BF16),
        ],
        compiler_params=pltpu.CompilerParams(vmem_limit_bytes=48 << 20),
        cost_estimate=pl.CostEstimate(
            flops=2 * rows * width * PROJ_WIDTH,
            bytes_accessed=2 * width * PROJ_WIDTH + 10 * rows * PROJ_WIDTH,
            transcendentals=0,
        ),
    )(place, xa, cosine, sine, gains, *[part for _, _, part in parts])


def unproject_kernel(layout, depth, relative, place_ref, grad_ref, *refs):
    weights, out_ref = refs[:-1], refs[-1]
    device = place_ref[1]
    across = (((1,), (1,)), ((), ()))
    for weight, (k, at, high) in zip(weights, layout):
        part = lax.dot_general(
            grad_ref[...], weight[...], across, preferred_element_type=F32
        )
        out_ref[:, pl.ds(block_start(k, at, depth, device, relative), high)] = part


def unproject(place, grad, entries, depth):
    rows = grad.shape[0]
    parts = laid_out(entries)
    layout = tuple((k, at, part.shape[0]) for k, at, part in parts)
    width = depth * len(entries)
    vmem = pl.BlockSpec(memory_space=pltpu.VMEM)
    return pl.pallas_call(
        partial(unproject_kernel, layout, depth, tuned()),
        in_specs=[pl.BlockSpec(memory_space=pltpu.SMEM)] + [vmem] * (1 + len(parts)),
        out_specs=vmem,
        out_shape=jax.ShapeDtypeStruct((rows, width), F32),
        compiler_params=pltpu.CompilerParams(vmem_limit_bytes=32 << 20),
        cost_estimate=pl.CostEstimate(
            flops=2 * rows * width * PROJ_WIDTH,
            bytes_accessed=2 * width * PROJ_WIDTH + 4 * rows * width,
            transcendentals=0,
        ),
    )(place, grad, *[part for _, _, part in parts])


def joint_kernel(heights, columns_ref, *refs):
    parts, out_ref = refs[:-1], refs[-1]
    total, at = None, 0
    for part, high in zip(parts, heights):
        term = lax.dot_general(
            columns_ref[at : at + high, :],
            part[...],
            (((0,), (0,)), ((), ())),
            preferred_element_type=F32,
        )
        total = term if total is None else total + term
        at += high
    out_ref[...] = total.astype(BF16)


def joint_product(columns, entries):
    parts = [part for entry in entries for part in entry]
    width = parts[0].shape[1]
    vmem = pl.BlockSpec(memory_space=pltpu.VMEM)
    return pl.pallas_call(
        partial(joint_kernel, tuple(part.shape[0] for part in parts)),
        in_specs=[vmem] * (1 + len(parts)),
        out_specs=vmem,
        out_shape=jax.ShapeDtypeStruct((columns.shape[1], width), BF16),
        compiler_params=pltpu.CompilerParams(vmem_limit_bytes=48 << 20),
        cost_estimate=pl.CostEstimate(
            flops=2 * columns.shape[0] * columns.shape[1] * width,
            bytes_accessed=2 * columns.shape[0] * width,
            transcendentals=0,
        ),
    )(columns, *parts)


def down_kernel(count, *refs):
    lefts, rights, outs = refs[:count], refs[count : 2 * count], refs[2 * count :]
    total = None
    for left, right in zip(lefts, rights):
        term = lax.dot_general(
            left[...], right[...], (((0,), (0,)), ((), ())), preferred_element_type=F32
        )
        total = term if total is None else total + term
    for j, out_ref in enumerate(outs):

        @pl.when(pl.program_id(0) == j)
        def _(out_ref=out_ref):
            out_ref[...] = total.astype(BF16)


def down_product(lefts, rights, cuts):
    rows, high = lefts[0].shape
    width = rights[0].shape[1] // cuts
    count = len(lefts)
    return pl.pallas_call(
        partial(down_kernel, count),
        grid=(cuts,),
        in_specs=[pl.BlockSpec((rows, high), lambda j: (0, 0))] * count
        + [pl.BlockSpec((rows, width), lambda j: (0, j))] * count,
        out_specs=[pl.BlockSpec((high, width), lambda j: (0, 0))] * cuts,
        out_shape=[jax.ShapeDtypeStruct((high, width), BF16)] * cuts,
        compiler_params=pltpu.CompilerParams(vmem_limit_bytes=56 << 20),
        cost_estimate=pl.CostEstimate(
            flops=2 * rows * count * high * width * cuts,
            bytes_accessed=4 * rows * count * (high + width),
            transcendentals=0,
        ),
    )(*lefts, *rights)


def gateup_kernel(count, place_ref, *refs):
    lefts, rights, outs = refs[:count], refs[count : 2 * count], refs[2 * count :]
    total = None
    for left, right in zip(lefts, rights):
        term = lax.dot_general(
            left[...], right[...], (((0,), (0,)), ((), ())), preferred_element_type=F32
        )
        total = term if total is None else total + term
    for j, out_ref in enumerate(outs):

        @pl.when(pl.program_id(0) // 2 == j)
        def _(out_ref=out_ref):
            out_ref[...] = total.astype(BF16)


def gateup_product(place, lefts, rights, depth, first, pairs):
    rows = lefts[0].shape[0]
    width = rights[0].shape[1]
    count = len(lefts)
    return pl.pallas_call(
        partial(gateup_kernel, count),
        grid_spec=pltpu.PrefetchScalarGridSpec(
            num_scalar_prefetch=1,
            grid=(2 * pairs,),
            in_specs=[
                pl.BlockSpec((rows, depth), lambda j, place: (0, place[1] ^ (first + j)))
            ]
            * count
            + [pl.BlockSpec((rows, width), lambda j, place: (0, 0))] * count,
            out_specs=[
                pl.BlockSpec(
                    (depth, width), lambda j, place, p=p: (jnp.clip(j - 2 * p, 0, 1), 0)
                )
                for p in range(pairs)
            ],
        ),
        out_shape=[jax.ShapeDtypeStruct((2 * depth, width), BF16)] * pairs,
        compiler_params=pltpu.CompilerParams(vmem_limit_bytes=56 << 20),
        cost_estimate=pl.CostEstimate(
            flops=4 * rows * count * depth * pairs * width,
            bytes_accessed=4 * rows * count * width,
            transcendentals=0,
        ),
    )(place, *lefts, *rights)


def collect_kernel(place_ref, *refs):
    pieces, out_ref = refs[:-1], refs[-1]
    depth = pieces[0].shape[0]
    for k, piece in enumerate(pieces):
        start = pl.multiple_of((place_ref[1] ^ k) * depth, depth)
        out_ref[pl.ds(start, depth), :] = piece[...]


def collect_rows(place, pieces):
    depth, width = pieces[0].shape
    vmem = pl.BlockSpec(memory_space=pltpu.VMEM)
    return pl.pallas_call(
        collect_kernel,
        in_specs=[pl.BlockSpec(memory_space=pltpu.SMEM)] + [vmem] * len(pieces),
        out_specs=vmem,
        out_shape=jax.ShapeDtypeStruct((depth * len(pieces), width), BF16),
        compiler_params=pltpu.CompilerParams(vmem_limit_bytes=16 << 20),
        cost_estimate=pl.CostEstimate(
            flops=0, bytes_accessed=4 * depth * len(pieces) * width, transcendentals=0
        ),
    )(place, *pieces)


def put_kernel(place_ref, piece_ref, *refs):
    refs[-1][...] = piece_ref[...].astype(F32)


def put_columns(place, whole, piece, k, units, size):
    rows = piece.shape[0]
    extra = [] if whole is None else [whole]
    return pl.pallas_call(
        put_kernel,
        grid_spec=pltpu.PrefetchScalarGridSpec(
            num_scalar_prefetch=1,
            grid=(2,),
            in_specs=[pl.BlockSpec((rows, units), lambda j, place: (0, j))]
            + [pl.BlockSpec(memory_space=pl.ANY)] * len(extra),
            out_specs=pl.BlockSpec(
                (rows, units), lambda j, place: (0, j * size + (place[1] ^ k))
            ),
        ),
        out_shape=jax.ShapeDtypeStruct((rows, 2 * units * size), F32),
        input_output_aliases={2: 0} if extra else {},
        compiler_params=pltpu.CompilerParams(vmem_limit_bytes=16 << 20),
        cost_estimate=pl.CostEstimate(
            flops=rows * units, bytes_accessed=12 * rows * units, transcendentals=0
        ),
    )(place, piece, *extra)


def hidden_kernel(layout, depth, tokens_ref, inputs_ref, gain_ref, *refs):
    count = len(layout)
    weights, (hidden_ref, low_ref) = refs[:count], refs[count : count + 2]
    held, semaphores = refs[count + 2 : 2 * count + 2], refs[2 * count + 2]
    copies = [
        pltpu.make_async_copy(weight, target, semaphores.at[j])
        for j, (weight, target) in enumerate(zip(weights, held))
    ]
    for copy in copies:
        copy.start()
    total = inputs_ref[...].astype(F32)
    for copy, target, (k, at, high) in zip(copies, held, layout):
        copy.wait()
        start = k * depth + at
        total = total + jnp.dot(
            tokens_ref[:, start : start + high], target[...], preferred_element_type=F32
        )
    hidden_ref[...] = total
    scale = lax.rsqrt(jnp.mean(total * total, axis=-1, keepdims=True) + EPSILON)
    low_ref[...] = (total * scale * gain_ref[...]).astype(BF16)


def add_heads(tokens, inputs, gain, entries):
    rows, width = inputs.shape
    parts = laid_out(entries)
    layout = tuple((k, at, part.shape[0]) for k, at, part in parts)
    depth = sum(part.shape[0] for part in entries[0])
    vmem = pl.BlockSpec(memory_space=pltpu.VMEM)
    return pl.pallas_call(
        partial(hidden_kernel, layout, depth),
        in_specs=[vmem] * 3 + [pl.BlockSpec(memory_space=pl.ANY)] * len(parts),
        out_specs=[vmem, vmem],
        out_shape=[
            jax.ShapeDtypeStruct((rows, width), F32),
            jax.ShapeDtypeStruct((rows, width), BF16),
        ],
        scratch_shapes=[pltpu.VMEM(part.shape, BF16) for _, _, part in parts]
        + [pltpu.SemaphoreType.DMA((len(parts),))],
        compiler_params=pltpu.CompilerParams(vmem_limit_bytes=48 << 20),
        cost_estimate=pl.CostEstimate(
            flops=2 * rows * width * QUERY_WIDTH,
            bytes_accessed=2 * width * QUERY_WIDTH + 8 * rows * width,
            transcendentals=0,
        ),
    )(tokens, inputs, gain[None, :], *[part for _, _, part in parts])


def head_at(place, span, device):
    if span is None:
        return place
    return (device ^ (place // span)) * span + place % span


def unpack_heads(source_ref, target, count, offset, row, scale=None, head=lambda h: h):
    rows = source_ref.shape[0]
    for h in range(count):
        part = source_ref[:, offset + h * HEAD_WIDTH : offset + (h + 1) * HEAD_WIDTH]
        if scale is not None:
            part = part * scale
        target[head(h), row : row + rows, :] = part


def stack_heads(source_ref, target, scale=None, head=lambda h: h):
    rows = source_ref.shape[0]
    for h in range(QUERY_HEADS):
        part = source_ref[:, h * HEAD_WIDTH : (h + 1) * HEAD_WIDTH]
        if scale is not None:
            part = part * scale
        at = pl.multiple_of((head(h) % GROUP) * rows, rows)
        target[head(h) // GROUP, pl.ds(at, rows), :] = part


def pack_heads(source, target_ref, count, head=lambda h: h):
    for h in range(0, count, 2):
        target_ref[:, h * HEAD_WIDTH : (h + 2) * HEAD_WIDTH] = jnp.concatenate(
            [source[head(h)], source[head(h + 1)]], axis=-1
        )


def attend_kernel(ranks, span, place_ref, begin_ref, query_ref, *refs):
    pairs, out_ref, log_ref = refs[:ranks], refs[ranks], refs[ranks + 1]
    queries, keys, values, outs, bias, logs = refs[ranks + 2 :]
    rows = query_ref.shape[0]
    rank, device = place_ref[0], place_ref[1]
    head = lambda h: head_at(h, span, device)
    stack_heads(query_ref, queries, jnp.asarray(SCALE, BF16))
    for r in range(ranks):
        unpack_heads(pairs[r], keys, KEY_VALUE_HEADS, 0, r * rows)
        unpack_heads(pairs[r], values, KEY_VALUE_HEADS, KEY_WIDTH, r * rows)
        key_at = (rank - r) * rows + lax.broadcasted_iota(jnp.int32, (rows, rows), 1)
        query_at = rank * rows + lax.broadcasted_iota(jnp.int32, (rows, rows), 0)
        allowed = (key_at <= query_at) & (key_at >= begin_ref[...])
        bias[:, r * rows : (r + 1) * rows] = jnp.where(allowed, 0.0, NEG_LARGE)
    logs[...] = jnp.zeros_like(logs)

    def one_group(group, carry):
        scores = lax.dot_general(
            queries[group], keys[group], (((1,), (1,)), ((), ())), preferred_element_type=F32
        ) + jnp.concatenate([bias[...]] * GROUP, axis=0)
        top = jnp.max(scores, axis=-1, keepdims=True)
        weight = jnp.exp(scores - top)
        total = jnp.sum(weight, axis=-1, keepdims=True)
        mixed = jnp.dot(weight.astype(BF16), values[group], preferred_element_type=F32)
        mixed = (mixed * (1.0 / total)).astype(BF16)
        log_total = top + jnp.log(total)
        for h in range(GROUP):
            at = slice(h * rows, (h + 1) * rows)
            outs[group * GROUP + h] = mixed[at, :]
            mine = lane_index(logs.shape) == group * GROUP + h
            logs[...] = jnp.where(mine, log_total[at, :], logs[...])
        return carry

    lax.fori_loop(0, KEY_VALUE_HEADS, one_group, 0)
    pack_heads(outs, out_ref, QUERY_HEADS, head)
    log_ref[...] = jnp.transpose(logs[...])


def attend(place, span, begin, query, pairs):
    rows = query.shape[0]
    ranks = len(pairs)
    vmem = pl.BlockSpec(memory_space=pltpu.VMEM)
    elements = QUERY_HEADS * rows * rows * ranks
    return pl.pallas_call(
        partial(attend_kernel, ranks, span),
        in_specs=[pl.BlockSpec(memory_space=pltpu.SMEM)] + [vmem] * (2 + ranks),
        out_specs=[vmem, vmem],
        out_shape=[
            jax.ShapeDtypeStruct((rows, QUERY_WIDTH), BF16),
            jax.ShapeDtypeStruct((LANES, rows), F32),
        ],
        scratch_shapes=[
            pltpu.VMEM((KEY_VALUE_HEADS, GROUP * rows, HEAD_WIDTH), BF16),
            pltpu.VMEM((KEY_VALUE_HEADS, ranks * rows, HEAD_WIDTH), BF16),
            pltpu.VMEM((KEY_VALUE_HEADS, ranks * rows, HEAD_WIDTH), BF16),
            pltpu.VMEM((QUERY_HEADS, rows, HEAD_WIDTH), BF16),
            pltpu.VMEM((rows, ranks * rows), F32),
            pltpu.VMEM((rows, LANES), F32),
        ],
        compiler_params=pltpu.CompilerParams(vmem_limit_bytes=48 << 20),
        cost_estimate=pl.CostEstimate(
            flops=16 * elements * HEAD_WIDTH,
            bytes_accessed=4 * rows * QUERY_WIDTH + 2 * ranks * rows * PAIR_WIDTH,
            transcendentals=elements,
        ),
    )(place, begin[:, None], query, *pairs)


def attend_back_kernel(
    ranks, span, place_ref, begin_ref, query_ref, out_ref, grad_ref, log_ref, *refs
):
    pairs, grad_query_ref, grad_pair_ref = refs[:ranks], refs[ranks], refs[ranks + 1]
    queries, keys, values, grads, grad_queries, grad_keys, grad_values, bias, logs, inners = refs[
        ranks + 2 :
    ]
    rows = query_ref.shape[0]
    rank, device = place_ref[0], place_ref[1]
    head = lambda h: head_at(h, span, device)
    across = (((1,), (1,)), ((), ()))
    stack_heads(query_ref, queries, jnp.asarray(SCALE, BF16))
    stack_heads(grad_ref, grads, head=head)
    for r in range(ranks):
        unpack_heads(pairs[r], keys, KEY_VALUE_HEADS, 0, r * rows)
        unpack_heads(pairs[r], values, KEY_VALUE_HEADS, KEY_WIDTH, r * rows)
        key_at = (rank - r) * rows + lax.broadcasted_iota(jnp.int32, (rows, rows), 0)
        query_at = rank * rows + lax.broadcasted_iota(jnp.int32, (rows, rows), 1)
        allowed = (key_at <= query_at) & (key_at >= begin_ref[...])
        bias[r * rows : (r + 1) * rows, :] = jnp.where(allowed, 0.0, NEG_LARGE)
    product = grad_ref[...].astype(F32) * out_ref[...].astype(F32)
    shape = (32, QUERY_WIDTH)
    mine = lane_index(shape) // HEAD_WIDTH == lax.broadcasted_iota(jnp.int32, shape, 0)
    inner = lax.dot_general(
        jnp.where(mine, 1.0, 0.0),
        product,
        across,
        precision=lax.Precision.HIGHEST,
        preferred_element_type=F32,
    )
    for h in range(QUERY_HEADS):
        logs[h // GROUP, :, (h % GROUP) * rows : (h % GROUP + 1) * rows] = log_ref[h : h + 1, :]
        at = pl.multiple_of((head(h) % GROUP) * rows, rows)
        inners[head(h) // GROUP, :, pl.ds(at, rows)] = inner[h : h + 1, :]

    def one_group(group, carry):
        query, grad = queries[group], grads[group]
        log_total, inner = logs[group], inners[group]
        total = jnp.zeros((HEAD_WIDTH, GROUP * rows), F32)
        for r in range(ranks):
            at = slice(r * rows, (r + 1) * rows)
            key = keys[group, at, :]
            scores = lax.dot_general(key, query, across, preferred_element_type=F32)
            mask = jnp.concatenate([bias[at, :]] * GROUP, axis=1)
            probability = jnp.exp(scores + mask - log_total)
            grad_prob = lax.dot_general(
                values[group, at, :], grad, across, preferred_element_type=F32
            )
            grad_score = (probability * (grad_prob - inner)).astype(BF16)
            grad_keys[group, at, :] = jnp.dot(grad_score, query, preferred_element_type=F32)
            grad_values[group, at, :] = jnp.dot(
                probability.astype(BF16), grad, preferred_element_type=F32
            )
            total += lax.dot_general(
                key, grad_score, (((0,), (0,)), ((), ())), preferred_element_type=F32
            )
        turned = (jnp.transpose(total) * SCALE).astype(BF16)
        for h in range(GROUP):
            grad_queries[group * GROUP + h] = turned[h * rows : (h + 1) * rows, :]
        return carry

    lax.fori_loop(0, KEY_VALUE_HEADS, one_group, 0)
    pack_heads(grad_queries, grad_query_ref, QUERY_HEADS)
    for r in range(ranks):
        for source, offset in ((grad_keys, 0), (grad_values, KEY_WIDTH)):
            for g in range(0, KEY_VALUE_HEADS, 2):
                at = offset + g * HEAD_WIDTH
                grad_pair_ref[r, :, at : at + 2 * HEAD_WIDTH] = jnp.concatenate(
                    [
                        source[g, r * rows : (r + 1) * rows, :],
                        source[g + 1, r * rows : (r + 1) * rows, :],
                    ],
                    axis=-1,
                ).astype(BF16)


def attend_back(place, span, begin, query, out, grad, log_total, pairs):
    rows = query.shape[0]
    ranks = len(pairs)
    vmem = pl.BlockSpec(memory_space=pltpu.VMEM)
    elements = QUERY_HEADS * rows * rows * ranks
    heads = pltpu.VMEM((QUERY_HEADS, rows, HEAD_WIDTH), BF16)
    one_row = pltpu.VMEM((KEY_VALUE_HEADS, 1, GROUP * rows), F32)
    stacked = pltpu.VMEM((KEY_VALUE_HEADS, GROUP * rows, HEAD_WIDTH), BF16)
    return pl.pallas_call(
        partial(attend_back_kernel, ranks, span),
        in_specs=[pl.BlockSpec(memory_space=pltpu.SMEM)] + [vmem] * (5 + ranks),
        out_specs=[vmem, vmem],
        out_shape=[
            jax.ShapeDtypeStruct((rows, QUERY_WIDTH), BF16),
            jax.ShapeDtypeStruct((ranks, rows, PAIR_WIDTH), BF16),
        ],
        scratch_shapes=[
            stacked,
            pltpu.VMEM((KEY_VALUE_HEADS, ranks * rows, HEAD_WIDTH), BF16),
            pltpu.VMEM((KEY_VALUE_HEADS, ranks * rows, HEAD_WIDTH), BF16),
            stacked,
            heads,
            pltpu.VMEM((KEY_VALUE_HEADS, ranks * rows, HEAD_WIDTH), F32),
            pltpu.VMEM((KEY_VALUE_HEADS, ranks * rows, HEAD_WIDTH), F32),
            pltpu.VMEM((ranks * rows, rows), F32),
            one_row,
            one_row,
        ],
        compiler_params=pltpu.CompilerParams(vmem_limit_bytes=56 << 20),
        cost_estimate=pl.CostEstimate(
            flops=40 * elements * HEAD_WIDTH,
            bytes_accessed=6 * rows * QUERY_WIDTH + 6 * ranks * rows * PAIR_WIDTH,
            transcendentals=elements,
        ),
    )(place, begin[None, :], query, out, grad, log_total, *pairs)


def unposition_kernel(query_ref, pair_ref, raw_ref, cosine_ref, sine_ref, gain_ref, out_ref, sum_ref):
    column = pl.program_id(0)
    tiles = raw_ref.shape[1] // LANES

    def back(source, tile, row):
        at = slice(tile * LANES, (tile + 1) * LANES)
        grad = source[:, at].astype(F32)
        raw = raw_ref[:, at]
        scale = head_scale(raw)
        grad = grad * cosine_ref[...] - turn(grad * sine_ref[...])
        total = jnp.sum(grad * raw * scale, axis=0, keepdims=True)
        grad = grad * gain_ref[row : row + 1, :]
        grad = scale * (grad - raw * scale * scale * head_mean(grad * raw))
        out_ref[:, at] = grad.astype(BF16)
        return total

    @pl.when(column == 0)
    def _():
        sum_ref[...] = jnp.zeros_like(sum_ref)

    @pl.when(column < 2)
    def _():
        sum_ref[0:1, :] += sum(back(query_ref, tile, 0) for tile in range(tiles))

    @pl.when(column == 2)
    def _():
        sum_ref[1:2, :] += sum(back(pair_ref, tile, 1) for tile in range(tiles // 2))
        out_ref[:, KEY_WIDTH:] = pair_ref[:, KEY_WIDTH:]


def unposition(grad_query, grad_pair, raw, cosine, sine, gains):
    rows = raw.shape[0]
    block = PAIR_WIDTH
    whole = lambda j: (0, 0)
    return pl.pallas_call(
        unposition_kernel,
        grid=(PROJ_WIDTH // block,),
        in_specs=[
            pl.BlockSpec((rows, block), lambda j: (0, jnp.minimum(j, 1))),
            pl.BlockSpec((rows, block), whole),
            pl.BlockSpec((rows, block), lambda j: (0, j)),
            pl.BlockSpec((rows, LANES), whole),
            pl.BlockSpec((rows, LANES), whole),
            pl.BlockSpec((8, LANES), whole),
        ],
        out_specs=[
            pl.BlockSpec((rows, block), lambda j: (0, j)),
            pl.BlockSpec((8, LANES), whole),
        ],
        out_shape=[
            jax.ShapeDtypeStruct((rows, PROJ_WIDTH), BF16),
            jax.ShapeDtypeStruct((8, LANES), F32),
        ],
        compiler_params=pltpu.CompilerParams(vmem_limit_bytes=32 << 20),
        cost_estimate=pl.CostEstimate(
            flops=40 * rows * PROJ_WIDTH, bytes_accessed=8 * rows * PROJ_WIDTH, transcendentals=0
        ),
    )(grad_query, grad_pair, raw, cosine, sine, gains)


def tail_kernel(count, *refs):
    mixed, down_ref, out_grad_ref = refs[:count], refs[count], refs[count + 1]
    even, odd_ref, held = refs[count + 2 : -2], refs[-2], refs[-1]
    k = pl.program_id(0)
    for j in range(count):

        @pl.when(k == j)
        def _(j=j):
            held[...] = mixed[j][...]

    part = jnp.dot(held[...], down_ref[...], preferred_element_type=F32).astype(BF16)
    rows = part.shape[0]
    for j in range(count // 2):

        @pl.when(k == 2 * j)
        def _(j=j):
            even[j][:rows, :] = part
            even[j][rows:, :] = out_grad_ref[...]

    @pl.when(k % 2 == 1)
    def _():
        odd_ref[0, :rows, :] = part
        odd_ref[0, rows:, :] = out_grad_ref[...]


def tail_product(mixed, down, out_grad):
    count = len(mixed)
    rows, units = mixed[0].shape
    width = down.shape[1]
    extra = out_grad.shape[0] // count
    high = rows + extra
    whole = lambda k: (0, 0)
    *even, odd = pl.pallas_call(
        partial(tail_kernel, count),
        grid=(count,),
        in_specs=[pl.BlockSpec((rows, units), whole)] * count
        + [
            pl.BlockSpec((units, width), whole),
            pl.BlockSpec((extra, width), lambda k: (k, 0)),
        ],
        out_specs=[pl.BlockSpec((high, width), whole)] * (count // 2)
        + [pl.BlockSpec((1, high, width), lambda k: (k // 2, 0, 0))],
        out_shape=[jax.ShapeDtypeStruct((high, width), BF16)] * (count // 2)
        + [jax.ShapeDtypeStruct((count // 2, high, width), BF16)],
        scratch_shapes=[pltpu.VMEM((rows, units), BF16)],
        compiler_params=pltpu.CompilerParams(vmem_limit_bytes=48 << 20),
        cost_estimate=pl.CostEstimate(
            flops=2 * rows * count * units * width,
            bytes_accessed=2 * count * high * width,
            transcendentals=0,
        ),
    )(*mixed, down, out_grad)
    return even, odd


def inverse_rms(values):
    return lax.rsqrt(jnp.mean(values * values, axis=-1, keepdims=True) + EPSILON)


def norm_back(grad_out, values, scale):
    return scale * (
        grad_out - values * scale * scale * jnp.mean(grad_out * values, axis=-1, keepdims=True)
    )


def rope_tables(position):
    half_size = HEAD_WIDTH // 2
    inverse_freq = jnp.exp(
        jnp.arange(half_size, dtype=F32) * (-2.0 * math.log(10000.0) / HEAD_WIDTH)
    )
    angle = position.astype(F32)[:, None] * inverse_freq[None, :]
    copies = LANES // half_size
    return (jnp.tile(jnp.cos(angle), (1, copies)), jnp.tile(jnp.sin(angle), (1, copies)))


def gain_rows(gain):
    wide = jnp.tile(gain.astype(F32), LANES // HEAD_WIDTH)
    return jnp.broadcast_to(wide[None, :], (8, LANES))


def layer(
    block_input,
    doc_starts,
    attn_gain,
    query_key_value_weight,
    query_gain,
    key_gain,
    out_weight,
    mlp_gain,
    gateup_weight,
    down_weight,
    cotangent,
):
    count, rows, width = block_input.shape
    assert count == 1
    size = lax.axis_size(FSDP)
    ranks = lax.axis_size(SEQ)
    me = lax.axis_index(FSDP)
    rank = lax.axis_index(SEQ)
    depth = query_key_value_weight.shape[0]
    units = down_weight.shape[0]
    span = out_weight.shape[0] // HEAD_WIDTH if tuned() else None
    contract = (((0,), (0,)), ((), ()))
    transposed = (((1,), (1,)), ((), ()))

    place = jnp.stack([rank, me])

    qkv_pieces = gather_finish(gather_start(query_key_value_weight))
    gain_pieces = gather_small(jnp.stack([attn_gain, mlp_gain]))
    out_held = gather_start(out_weight)

    def gateup_columns(half, k):
        at = (half * size + peer(k)) * units
        return lax.dynamic_slice_in_dim(gateup_weight, at, units, axis=1)

    if tuned():
        even = rank % 2 == 0
        fetched = exchange([gateup_columns(rank % 2, k) for k in range(size)])
        mine = collect_rows(place, fetched)
        other = seq_move(mine, [(0, 1), (1, 0), (2, 3), (3, 2)])
        gateup_mine = jnp.concatenate(
            [jnp.where(even, mine, other), jnp.where(even, other, mine)], axis=1
        )
    else:
        gateup_mine = rows_to_absolute(
            exchange(
                [
                    jnp.concatenate([gateup_columns(0, k), gateup_columns(1, k)], axis=1)
                    for k in range(size)
                ],
            )
        )
    grad_low = cotangent.reshape(rows, width)
    grad_held = gather_start(grad_low)

    position = rank * rows + jnp.arange(rows, dtype=jnp.int32)
    starts = doc_starts.reshape(-1)
    begin = jnp.max(
        jnp.where(starts[None, :] <= position[:, None], starts[None, :], 0), axis=-1
    )
    cosine, sine = rope_tables(position - begin)
    query_gains, key_gains = gain_rows(query_gain), gain_rows(key_gain)

    tokens_in = block_input.reshape(rows, width)
    inputs = tokens_in.astype(F32)
    scale_attn = inverse_rms(inputs)
    order = peer(jnp.arange(size))
    gain_attn = gain_pieces[:, 0][order].reshape(width).astype(F32)
    gain_mlp = gain_pieces[:, 1][order].reshape(width).astype(F32)
    normed_low = (inputs * scale_attn * gain_attn).astype(BF16)
    mix_gains = jnp.concatenate([query_gains[:1], key_gains[:1], query_gains[:6]], axis=0)
    raw, query, pair, split = project(place, normed_low, cosine, sine, mix_gains, qkv_pieces, depth)
    pairs = [pair]
    for d in range(1, ranks):
        pairs.append(seq_move(pair, [(j, j + d) for j in range(ranks - d)]))
    out_pieces = gather_finish(out_held, pair)
    attn_tok, log_total = attend(place, span, begin, query, pairs)
    hidden, mlp_low = add_heads(attn_tok, tokens_in, gain_mlp, out_pieces)

    mlp_held = gather_start(mlp_low)
    mixed, grads_gu, parts = [], [], []
    grad_pieces = joined(gather_finish(grad_held, mlp_low))
    mlp_pieces = list(mlp_held[:2]) if tuned() else joined(gather_finish(mlp_held))
    for k in range(size):
        if tuned() and k == 2:
            mlp_pieces += joined(gather_finish(mlp_held, parts[1])[2:])
        if k:
            (mlp_pieces[k],) = after((mlp_pieces[k],), parts[k - 1])
        grad_here = lax.optimization_barrier(
            lax.dot_general(
                grad_pieces[k], down_weight, transposed, preferred_element_type=F32
            )
        )
        gate_up = jnp.dot(mlp_pieces[k], gateup_mine, preferred_element_type=F32)
        gate = gate_up[:, :units]
        upper = gate_up[:, units:]
        sigmoid_gate = jax.nn.sigmoid(gate)
        activated = gate * sigmoid_gate
        mixed.append((activated * upper).astype(BF16))
        grad_gate = grad_here * upper * sigmoid_gate * (1.0 + gate * (1.0 - sigmoid_gate))
        grad_upper = grad_here * activated
        grads_gu.append(jnp.concatenate([grad_gate, grad_upper], axis=-1).astype(BF16))
        parts.append(
            lax.dot_general(
                grads_gu[k], gateup_mine, transposed, preferred_element_type=F32
            ).astype(BF16)
        )
    grad_mlp_in = scatter_sum(parts)

    if tuned():
        down_cuts = down_product(mixed, grad_pieces, 2)
        gateup_parts = gateup_product(place, mlp_pieces, grads_gu, depth, 0, 2)
        gateup_parts += gateup_product(place, mlp_pieces, grads_gu, depth, 4, 2)
    else:
        mixed_low = jnp.concatenate(mixed, axis=0)
        down_cuts = [
            lax.dot_general(
                mixed_low,
                jnp.concatenate(grad_pieces, axis=0),
                contract,
                preferred_element_type=F32,
            ).astype(BF16)
        ]
        grad_gateup = lax.dot_general(
            jnp.concatenate(mlp_pieces, axis=0),
            jnp.concatenate(grads_gu, axis=0),
            contract,
            preferred_element_type=F32,
        ).astype(BF16)
        gateup_parts = [grad_gateup[k * depth : (k + 1) * depth] for k in range(size)]
    total_down = jnp.concatenate([seq_sum(cut) for cut in down_cuts], axis=1).astype(F32)
    if tuned():
        total_gateup = summed = None
        for p in reversed(range(len(gateup_parts))):
            part = gateup_parts[p]
            summed = seq_sum(part, summed)
            for k in (2 * p, 2 * p + 1):
                piece = summed[(k % 2) * depth : (k % 2 + 1) * depth]
                piece = swap(piece, k) if k else piece
                total_gateup = put_columns(place, total_gateup, piece, k, units, size)
    else:
        total_gateup = jnp.zeros((depth, 2 * units * size), F32)
        for k, part in enumerate(exchange(gateup_parts)):
            summed = seq_sum(part).astype(F32)
            for half in range(2):
                total_gateup = lax.dynamic_update_slice(
                    total_gateup,
                    summed[:, half * units : (half + 1) * units],
                    (0, (half * size + k) * units),
                )

    (hidden,) = after((hidden,), parts[0])
    scale_mlp = inverse_rms(hidden)
    grad_hidden = grad_low.astype(F32) + norm_back(
        grad_mlp_in * gain_mlp, hidden, scale_mlp
    )
    grad_mlp_gain = jnp.sum(grad_mlp_in * hidden * scale_mlp, axis=0)
    grad_hidden_low = grad_hidden.astype(BF16)

    out_all = jnp.concatenate(
        after([part for entry in out_pieces for part in entry], mlp_low), axis=0
    )
    grad_attn_low = lax.dot_general(
        grad_hidden_low, out_all, transposed, preferred_element_type=F32
    ).astype(BF16)
    grad_query, grad_pairs = attend_back(
        place, span, begin, query, attn_tok, grad_attn_low, log_total, pairs
    )
    back_pairs = [(j + 1, j) for j in range(ranks - 1)]
    carry = grad_pairs[ranks - 1]
    for r in range(ranks - 2, -1, -1):
        carry = add_low(grad_pairs[r], seq_move(carry, back_pairs))
    grad_proj, gain_sums = unposition(grad_query, carry, raw, cosine, sine, mix_gains)
    columns = exchange_tokens(split)
    entries = gather_direct(grad_proj)
    grad_weight = joint_product(columns, entries)
    total_qkv = seq_sum(grad_weight).astype(F32)

    late_tok, late_low = after((attn_tok, grad_hidden_low), grad_query)
    grad_out = lax.dot_general(
        late_tok, late_low, contract, preferred_element_type=F32
    ).astype(BF16)
    held = out_weight.shape[0]
    if tuned():
        late_mixed = after(mixed, grad_query)
        even, odd = tail_product(late_mixed, down_weight, grad_out)
        sums = scatter_direct(even, odd)
        out_sum, shard_out = sums[:rows], sums[rows:]
    else:
        shard_out = scatter_sum([grad_out[k * held : (k + 1) * held] for k in range(size)])
        out_sum = scatter_sum(
            [jnp.dot(m, down_weight, preferred_element_type=F32).astype(BF16) for m in mixed]
        )
    total_out = seq_sum(shard_out.astype(BF16)).astype(F32)
    (late_hidden,) = after((hidden,), grad_query)
    block_output = (late_hidden + out_sum).astype(BF16).reshape(block_input.shape)

    grad_attn_in = unproject(place, grad_proj, qkv_pieces, depth)
    grad_attn_gain = jnp.sum(grad_attn_in * (inputs * scale_attn), axis=0)
    input_grad = grad_hidden + norm_back(grad_attn_in * gain_attn, inputs, scale_attn)

    small = jnp.concatenate([grad_attn_gain, grad_mlp_gain, gain_sums[0], gain_sums[1]])
    small = sum_small(small)
    total_attn_gain = lax.dynamic_slice_in_dim(small, me * depth, depth)
    total_mlp_gain = lax.dynamic_slice_in_dim(small, width + me * depth, depth)
    heads = small[2 * width :].reshape(2, LANES // HEAD_WIDTH, HEAD_WIDTH).sum(axis=1)
    return (
        block_output,
        input_grad.reshape(block_input.shape),
        total_attn_gain,
        total_qkv,
        heads[0],
        heads[1],
        total_out,
        total_mlp_gain,
        total_gateup,
        total_down,
    )


def solution(mesh):
    return jax.shard_map(
        layer,
        mesh=mesh,
        in_specs=(
            P(FSDP, SEQ, None),
            P(FSDP, None),
            P(FSDP),
            P(FSDP, None),
            P(),
            P(),
            P(FSDP, None),
            P(FSDP),
            P(FSDP, None),
            P(FSDP, None),
            P(FSDP, SEQ, None),
        ),
        out_specs=(
            P(FSDP, SEQ, None),
            P(FSDP, SEQ, None),
            P(FSDP),
            P(FSDP, None),
            P(),
            P(),
            P(FSDP, None),
            P(FSDP),
            P(FSDP, None),
            P(FSDP, None),
        ),
        check_vma=False,
    )
```

```python
from functools import partial
import math

import jax
import jax.numpy as jnp
from jax import lax
from jax.experimental import pallas as pl
from jax.experimental.pallas import tpu as pltpu
from jax.sharding import PartitionSpec as P


QUERY_HEADS = 24
KEY_VALUE_HEADS = 6
HEAD_WIDTH = 64
GROUP = QUERY_HEADS // KEY_VALUE_HEADS
QUERY_WIDTH = QUERY_HEADS * HEAD_WIDTH
KEY_WIDTH = KEY_VALUE_HEADS * HEAD_WIDTH
PAIR_WIDTH = 2 * KEY_WIDTH
PROJ_WIDTH = QUERY_WIDTH + PAIR_WIDTH
LANES = 128
FSDP, SEQ = "fsdp", "seq"

EPSILON = 1e-06
NEG_LARGE = -1e30
SCALE = HEAD_WIDTH ** (-0.5)


F32 = jnp.float32
BF16 = jnp.bfloat16


def tuned():
    return lax.axis_size(FSDP) == 8 and lax.axis_size(SEQ) == 4


def peer(k):
    return lax.axis_index(FSDP) ^ k if tuned() else k


def swap(block, distance):
    size = lax.axis_size(FSDP)
    return lax.ppermute(block, FSDP, [(i, i ^ distance) for i in range(size)])


def seq_move(value, pairs):
    return lax.ppermute(value, SEQ, pairs)


def after(values, gate):
    return lax.optimization_barrier((*values, gate))[:-1]


def gather_start(block):
    if not tuned():
        return lax.all_gather(block, FSDP, axis=0)
    return (block, swap(block, 1), swap(block, 2), swap(block, 4))


def gather_finish(held, gate=None):
    if not tuned():
        return [(held[k],) for k in range(held.shape[0])]
    block, core, across, along = held
    if gate is not None:
        across, along = after((across, along), gate)
    half = block.shape[0] // 2
    low = swap(along[:half], 2)
    high = swap(across[half:], 4)
    across_core = swap(across, 1)
    along_core = swap(along, 1)
    low_core = swap(low, 1)
    high_core = swap(high, 1)
    return [
        (block,),
        (core,),
        (across,),
        (across_core,),
        (along,),
        (along_core,),
        (low, high),
        (low_core, high_core),
    ]


def gather_direct(block):
    if not tuned():
        return gather_finish(gather_start(block))
    core = swap(block, 1)
    across = swap(block, 2)
    along = swap(block, 4)
    diagonal = swap(block, 6)
    pieces = [block, core]
    for part in (across, along, diagonal):
        pieces += [part, swap(part, 1)]
    return [(piece,) for piece in pieces]


def joined(entries):
    return [e[0] if len(e) == 1 else jnp.concatenate(e, axis=0) for e in entries]


def laid_out(entries):
    out = []
    for k, entry in enumerate(entries):
        at = 0
        for part in entry:
            out.append((k, at, part))
            at += part.shape[0]
    return out


def gather_small(block):
    if not tuned():
        return lax.all_gather(block, FSDP, axis=0)
    held = block[None]
    for distance in (1, 2, 4):
        held = jnp.concatenate([held, swap(held, distance)], axis=0)
    return held


def add_low(left, right):
    return (left.astype(F32) + right.astype(F32)).astype(BF16)


def scatter_sum(blocks):
    if not tuned():
        held = jnp.concatenate(blocks)
        held = lax.psum_scatter(held, FSDP, scatter_dimension=0, tiled=True)
        return held.astype(F32)
    half = blocks[0].shape[0] // 2
    from_core = [swap(blocks[2 * k + 1], 1) for k in range(4)]
    across = add_low(blocks[2], from_core[1])
    across_low = swap(across[:half], 2)
    along = add_low(blocks[4], from_core[2])
    along_high = swap(along[half:], 4)
    diag = add_low(blocks[6], from_core[3])
    low = swap(diag[:half], 2)
    high = swap(diag[half:], 4)
    across_high = swap(add_low(across[half:], high), 2)
    along_low = swap(add_low(along[:half], low), 4)
    own = blocks[0].astype(F32) + from_core[0].astype(F32)
    from_across = jnp.concatenate([across_low, across_high], axis=0)
    from_along = jnp.concatenate([along_low, along_high], axis=0)
    return own + from_across.astype(F32) + from_along.astype(F32)


def scatter_direct(even, odd):
    came = swap(odd, 1)
    own, across, along, diagonal = (add_low(even[j], came[j]) for j in range(4))
    across = swap(across, 2)
    along = swap(along, 4)
    diagonal = swap(diagonal, 6)
    return own.astype(F32) + across.astype(F32) + along.astype(F32) + diagonal.astype(F32)


def exchange(blocks):
    size = len(blocks)
    if tuned():
        return [blocks[0]] + [swap(blocks[k], k) for k in range(1, size)]
    held = lax.all_to_all(jnp.stack(blocks), FSDP, 0, 0)
    return [held[k] for k in range(size)]


def exchange_tokens(held):
    if not tuned():
        return lax.all_to_all(held, FSDP, 0, 0).reshape(-1, held.shape[2])
    came = None
    for distance in (1, 2, 4):
        if came is not None:
            held = jnp.concatenate([split[:, 0], came], axis=1)
        split = held.reshape((-1, 2) + held.shape[1:])
        leaving = split[:, 1]
        came = swap(leaving, distance)
    return jnp.concatenate([split[:, 0], came], axis=1)[0]


def seq_sum(value, gate=None):
    if not tuned():
        return lax.psum(value, SEQ)
    rank = lax.axis_index(SEQ)
    first = add_low(value, seq_move(value, [(0, 1), (3, 2)]))
    other = seq_move(first, [(1, 2), (2, 1)])
    total = add_low(first, other)
    ends = seq_move(total, [(1, 0), (2, 3)])
    if gate is not None:
        total, ends = after((total, ends), gate)
    return jnp.where((rank == 1) | (rank == 2), total, ends)


def sum_small(values):
    if not tuned():
        return lax.psum(values, (FSDP, SEQ))
    values = values.reshape(-1, LANES)
    for distance in (1, 2, 4):
        came = swap(values, distance)
        values = values + came
    for distance in (1, 2):
        pairs = [(j, j ^ distance) for j in range(4)]
        came = seq_move(values, pairs)
        values = values + came
    return values.reshape(-1)


def rows_to_absolute(pieces):
    depth = pieces[0].shape[0]
    whole = jnp.zeros((depth * len(pieces),) + pieces[0].shape[1:], pieces[0].dtype)
    for k, piece in enumerate(pieces):
        whole = lax.dynamic_update_slice_in_dim(whole, piece, peer(k) * depth, axis=0)
    return whole


def lane_index(shape):
    return lax.broadcasted_iota(jnp.int32, shape, 1)


def head_scale(values):
    low = lane_index(values.shape) < HEAD_WIDTH
    squares = values * values
    first = jnp.sum(jnp.where(low, squares, 0.0), axis=-1, keepdims=True)
    second = jnp.sum(jnp.where(low, 0.0, squares), axis=-1, keepdims=True)
    return jnp.where(
        low,
        lax.rsqrt(first * (1.0 / HEAD_WIDTH) + EPSILON),
        lax.rsqrt(second * (1.0 / HEAD_WIDTH) + EPSILON),
    )


def head_mean(values):
    low = lane_index(values.shape) < HEAD_WIDTH
    first = jnp.sum(jnp.where(low, values, 0.0), axis=-1, keepdims=True)
    second = jnp.sum(jnp.where(low, 0.0, values), axis=-1, keepdims=True)
    return jnp.where(low, first, second) * (1.0 / HEAD_WIDTH)


def turn(values):
    half = HEAD_WIDTH // 2
    first = (lane_index(values.shape) % HEAD_WIDTH) < half
    return jnp.where(
        first, -pltpu.roll(values, LANES - half, 1), pltpu.roll(values, half, 1)
    )


def block_start(k, at, depth, device, relative):
    if not relative:
        return k * depth + at
    return pl.multiple_of((device ^ k) * depth + at, LANES)


def project_kernel(layout, depth, relative, place_ref, xa_ref, cosine_ref, sine_ref, gain_ref, *refs):
    count = len(layout)
    weights, (raw_ref, query_ref, pair_ref, split_ref) = refs[:count], refs[count:]
    device = place_ref[1]
    total = None
    for weight, (k, at, high) in zip(weights, layout):
        left = xa_ref[:, pl.ds(block_start(k, at, depth, device, relative), high)]
        term = jnp.dot(left, weight[...], preferred_element_type=F32)
        total = term if total is None else total + term
        split_ref[k, :, at : at + high] = left
    raw_ref[...] = total
    column = pl.program_id(0)
    tiles = total.shape[1] // LANES

    def positioned(tile, gain):
        part = total[:, tile * LANES : (tile + 1) * LANES]
        normed = part * head_scale(part) * gain
        return (normed * cosine_ref[...] + turn(normed) * sine_ref[...]).astype(BF16)

    @pl.when(column < 2)
    def _():
        for tile in range(tiles):
            query_ref[:, tile * LANES : (tile + 1) * LANES] = positioned(tile, gain_ref[0:1, :])

    @pl.when(column == 2)
    def _():
        for tile in range(tiles // 2):
            pair_ref[:, tile * LANES : (tile + 1) * LANES] = positioned(tile, gain_ref[1:2, :])
        pair_ref[:, KEY_WIDTH:] = total[:, KEY_WIDTH:].astype(BF16)


def project(place, xa, cosine, sine, gains, entries, depth):
    rows, width = xa.shape
    block = PAIR_WIDTH
    parts = laid_out(entries)
    layout = tuple((k, at, part.shape[0]) for k, at, part in parts)
    whole = lambda j: (0, 0)
    return pl.pallas_call(
        partial(project_kernel, layout, depth, tuned()),
        grid=(PROJ_WIDTH // block,),
        in_specs=[
            pl.BlockSpec(memory_space=pltpu.SMEM),
            pl.BlockSpec((rows, width), whole),
            pl.BlockSpec((rows, LANES), whole),
            pl.BlockSpec((rows, LANES), whole),
            pl.BlockSpec((8, LANES), whole),
        ]
        + [pl.BlockSpec((part.shape[0], block), lambda j: (0, j)) for _, _, part in parts],
        out_specs=[
            pl.BlockSpec((rows, block), lambda j: (0, j)),
            pl.BlockSpec((rows, block), lambda j: (0, jnp.minimum(j, 1))),
            pl.BlockSpec((rows, block), whole),
            pl.BlockSpec((len(entries), rows, depth), lambda j: (0, 0, 0)),
        ],
        out_shape=[
            jax.ShapeDtypeStruct((rows, PROJ_WIDTH), F32),
            jax.ShapeDtypeStruct((rows, QUERY_WIDTH), BF16),
            jax.ShapeDtypeStruct((rows, PAIR_WIDTH), BF16),
            jax.ShapeDtypeStruct((len(entries), rows, depth), BF16),
        ],
        compiler_params=pltpu.CompilerParams(vmem_limit_bytes=48 << 20),
        cost_estimate=pl.CostEstimate(
            flops=2 * rows * width * PROJ_WIDTH,
            bytes_accessed=2 * width * PROJ_WIDTH + 10 * rows * PROJ_WIDTH,
            transcendentals=0,
        ),
    )(place, xa, cosine, sine, gains, *[part for _, _, part in parts])


def unproject_kernel(layout, depth, relative, place_ref, grad_ref, *refs):
    weights, out_ref = refs[:-1], refs[-1]
    device = place_ref[1]
    across = (((1,), (1,)), ((), ()))
    for weight, (k, at, high) in zip(weights, layout):
        part = lax.dot_general(
            grad_ref[...], weight[...], across, preferred_element_type=F32
        )
        out_ref[:, pl.ds(block_start(k, at, depth, device, relative), high)] = part


def unproject(place, grad, entries, depth):
    rows = grad.shape[0]
    parts = laid_out(entries)
    layout = tuple((k, at, part.shape[0]) for k, at, part in parts)
    width = depth * len(entries)
    vmem = pl.BlockSpec(memory_space=pltpu.VMEM)
    return pl.pallas_call(
        partial(unproject_kernel, layout, depth, tuned()),
        in_specs=[pl.BlockSpec(memory_space=pltpu.SMEM)] + [vmem] * (1 + len(parts)),
        out_specs=vmem,
        out_shape=jax.ShapeDtypeStruct((rows, width), F32),
        compiler_params=pltpu.CompilerParams(vmem_limit_bytes=32 << 20),
        cost_estimate=pl.CostEstimate(
            flops=2 * rows * width * PROJ_WIDTH,
            bytes_accessed=2 * width * PROJ_WIDTH + 4 * rows * width,
            transcendentals=0,
        ),
    )(place, grad, *[part for _, _, part in parts])


def joint_kernel(heights, columns_ref, *refs):
    parts, out_ref = refs[:-1], refs[-1]
    total, at = None, 0
    for part, high in zip(parts, heights):
        term = lax.dot_general(
            columns_ref[at : at + high, :],
            part[...],
            (((0,), (0,)), ((), ())),
            preferred_element_type=F32,
        )
        total = term if total is None else total + term
        at += high
    out_ref[...] = total.astype(BF16)


def joint_product(columns, entries):
    parts = [part for entry in entries for part in entry]
    width = parts[0].shape[1]
    vmem = pl.BlockSpec(memory_space=pltpu.VMEM)
    return pl.pallas_call(
        partial(joint_kernel, tuple(part.shape[0] for part in parts)),
        in_specs=[vmem] * (1 + len(parts)),
        out_specs=vmem,
        out_shape=jax.ShapeDtypeStruct((columns.shape[1], width), BF16),
        compiler_params=pltpu.CompilerParams(vmem_limit_bytes=48 << 20),
        cost_estimate=pl.CostEstimate(
            flops=2 * columns.shape[0] * columns.shape[1] * width,
            bytes_accessed=2 * columns.shape[0] * width,
            transcendentals=0,
        ),
    )(columns, *parts)


def down_kernel(count, *refs):
    lefts, rights, outs = refs[:count], refs[count : 2 * count], refs[2 * count :]
    total = None
    for left, right in zip(lefts, rights):
        term = lax.dot_general(
            left[...], right[...], (((0,), (0,)), ((), ())), preferred_element_type=F32
        )
        total = term if total is None else total + term
    for j, out_ref in enumerate(outs):

        @pl.when(pl.program_id(0) == j)
        def _(out_ref=out_ref):
            out_ref[...] = total.astype(BF16)


def down_product(lefts, rights, cuts):
    rows, high = lefts[0].shape
    width = rights[0].shape[1] // cuts
    count = len(lefts)
    return pl.pallas_call(
        partial(down_kernel, count),
        grid=(cuts,),
        in_specs=[pl.BlockSpec((rows, high), lambda j: (0, 0))] * count
        + [pl.BlockSpec((rows, width), lambda j: (0, j))] * count,
        out_specs=[pl.BlockSpec((high, width), lambda j: (0, 0))] * cuts,
        out_shape=[jax.ShapeDtypeStruct((high, width), BF16)] * cuts,
        compiler_params=pltpu.CompilerParams(vmem_limit_bytes=56 << 20),
        cost_estimate=pl.CostEstimate(
            flops=2 * rows * count * high * width * cuts,
            bytes_accessed=4 * rows * count * (high + width),
            transcendentals=0,
        ),
    )(*lefts, *rights)


def gateup_kernel(count, place_ref, *refs):
    lefts, rights, outs = refs[:count], refs[count : 2 * count], refs[2 * count :]
    total = None
    for left, right in zip(lefts, rights):
        term = lax.dot_general(
            left[...], right[...], (((0,), (0,)), ((), ())), preferred_element_type=F32
        )
        total = term if total is None else total + term
    for j, out_ref in enumerate(outs):

        @pl.when(pl.program_id(0) == j)
        def _(out_ref=out_ref):
            out_ref[...] = total.astype(BF16)


def gateup_product(place, lefts, rights, depth, first, pairs):
    rows = lefts[0].shape[0]
    width = rights[0].shape[1]
    count = len(lefts)
    return pl.pallas_call(
        partial(gateup_kernel, count),
        grid_spec=pltpu.PrefetchScalarGridSpec(
            num_scalar_prefetch=1,
            grid=(pairs,),
            in_specs=[
                pl.BlockSpec(
                    (rows, 2 * depth), lambda j, place: (0, (place[1] // 2) ^ (first + j))
                )
            ]
            * count
            + [pl.BlockSpec((rows, width), lambda j, place: (0, 0))] * count,
            out_specs=[pl.BlockSpec((2 * depth, width), lambda j, place: (0, 0))] * pairs,
        ),
        out_shape=[jax.ShapeDtypeStruct((2 * depth, width), BF16)] * pairs,
        compiler_params=pltpu.CompilerParams(vmem_limit_bytes=56 << 20),
        cost_estimate=pl.CostEstimate(
            flops=4 * rows * count * depth * pairs * width,
            bytes_accessed=4 * rows * count * width,
            transcendentals=0,
        ),
    )(place, *lefts, *rights)


def collect_kernel(place_ref, *refs):
    pieces, out_ref = refs[:-1], refs[-1]
    depth = pieces[0].shape[0]
    for k, piece in enumerate(pieces):
        start = pl.multiple_of((place_ref[1] ^ k) * depth, depth)
        out_ref[pl.ds(start, depth), :] = piece[...]


def collect_rows(place, pieces):
    depth, width = pieces[0].shape
    vmem = pl.BlockSpec(memory_space=pltpu.VMEM)
    return pl.pallas_call(
        collect_kernel,
        in_specs=[pl.BlockSpec(memory_space=pltpu.SMEM)] + [vmem] * len(pieces),
        out_specs=vmem,
        out_shape=jax.ShapeDtypeStruct((depth * len(pieces), width), BF16),
        compiler_params=pltpu.CompilerParams(vmem_limit_bytes=16 << 20),
        cost_estimate=pl.CostEstimate(
            flops=0, bytes_accessed=4 * depth * len(pieces) * width, transcendentals=0
        ),
    )(place, *pieces)


def put_kernel(place_ref, piece_ref, *refs):
    refs[-1][...] = piece_ref[...].astype(F32)


def put_columns(place, whole, piece, k, units, size):
    rows = piece.shape[0]
    extra = [] if whole is None else [whole]
    return pl.pallas_call(
        put_kernel,
        grid_spec=pltpu.PrefetchScalarGridSpec(
            num_scalar_prefetch=1,
            grid=(2,),
            in_specs=[pl.BlockSpec((rows, units), lambda j, place: (0, j))]
            + [pl.BlockSpec(memory_space=pl.ANY)] * len(extra),
            out_specs=pl.BlockSpec(
                (rows, units), lambda j, place: (0, j * size + (place[1] ^ k))
            ),
        ),
        out_shape=jax.ShapeDtypeStruct((rows, 2 * units * size), F32),
        input_output_aliases={2: 0} if extra else {},
        compiler_params=pltpu.CompilerParams(vmem_limit_bytes=16 << 20),
        cost_estimate=pl.CostEstimate(
            flops=rows * units, bytes_accessed=12 * rows * units, transcendentals=0
        ),
    )(place, piece, *extra)


def hidden_kernel(layout, depth, tokens_ref, inputs_ref, gain_ref, *refs):
    count = len(layout)
    weights, (hidden_ref, low_ref) = refs[:count], refs[count : count + 2]
    held, semaphores = refs[count + 2 : 2 * count + 2], refs[2 * count + 2]
    copies = [
        pltpu.make_async_copy(weight, target, semaphores.at[j])
        for j, (weight, target) in enumerate(zip(weights, held))
    ]
    for copy in copies:
        copy.start()
    total = inputs_ref[...].astype(F32)
    for copy, target, (k, at, high) in zip(copies, held, layout):
        copy.wait()
        start = k * depth + at
        total = total + jnp.dot(
            tokens_ref[:, start : start + high], target[...], preferred_element_type=F32
        )
    hidden_ref[...] = total
    scale = lax.rsqrt(jnp.mean(total * total, axis=-1, keepdims=True) + EPSILON)
    low_ref[...] = (total * scale * gain_ref[...]).astype(BF16)


def add_heads(tokens, inputs, gain, entries):
    rows, width = inputs.shape
    parts = laid_out(entries)
    layout = tuple((k, at, part.shape[0]) for k, at, part in parts)
    depth = sum(part.shape[0] for part in entries[0])
    vmem = pl.BlockSpec(memory_space=pltpu.VMEM)
    return pl.pallas_call(
        partial(hidden_kernel, layout, depth),
        in_specs=[vmem] * 3 + [pl.BlockSpec(memory_space=pl.ANY)] * len(parts),
        out_specs=[vmem, vmem],
        out_shape=[
            jax.ShapeDtypeStruct((rows, width), F32),
            jax.ShapeDtypeStruct((rows, width), BF16),
        ],
        scratch_shapes=[pltpu.VMEM(part.shape, BF16) for _, _, part in parts]
        + [pltpu.SemaphoreType.DMA((len(parts),))],
        compiler_params=pltpu.CompilerParams(vmem_limit_bytes=48 << 20),
        cost_estimate=pl.CostEstimate(
            flops=2 * rows * width * QUERY_WIDTH,
            bytes_accessed=2 * width * QUERY_WIDTH + 8 * rows * width,
            transcendentals=0,
        ),
    )(tokens, inputs, gain[None, :], *[part for _, _, part in parts])


def head_at(place, span, device):
    if span is None:
        return place
    return (device ^ (place // span)) * span + place % span


def unpack_heads(source_ref, target, count, offset, row, scale=None, head=lambda h: h):
    rows = source_ref.shape[0]
    for h in range(count):
        part = source_ref[:, offset + h * HEAD_WIDTH : offset + (h + 1) * HEAD_WIDTH]
        if scale is not None:
            part = part * scale
        target[head(h), row : row + rows, :] = part


def stack_heads(source_ref, target, scale=None, head=lambda h: h):
    rows = source_ref.shape[0]
    for h in range(QUERY_HEADS):
        part = source_ref[:, h * HEAD_WIDTH : (h + 1) * HEAD_WIDTH]
        if scale is not None:
            part = part * scale
        at = pl.multiple_of((head(h) % GROUP) * rows, rows)
        target[head(h) // GROUP, pl.ds(at, rows), :] = part


def pack_heads(source, target_ref, count, head=lambda h: h):
    for h in range(0, count, 2):
        target_ref[:, h * HEAD_WIDTH : (h + 2) * HEAD_WIDTH] = jnp.concatenate(
            [source[head(h)], source[head(h + 1)]], axis=-1
        )


def attend_kernel(ranks, span, place_ref, begin_ref, query_ref, *refs):
    pairs, out_ref, log_ref = refs[:ranks], refs[ranks], refs[ranks + 1]
    queries, keys, values, outs, bias = refs[ranks + 2 :]
    rows = query_ref.shape[0]
    rank, device = place_ref[0], place_ref[1]
    head = lambda h: head_at(h, span, device)
    across = (((1,), (1,)), ((), ()))
    stack_heads(query_ref, queries, jnp.asarray(SCALE, BF16))
    for r in range(ranks):
        unpack_heads(pairs[r], keys, KEY_VALUE_HEADS, 0, r * rows)
        unpack_heads(pairs[r], values, KEY_VALUE_HEADS, KEY_WIDTH, r * rows)
        key_at = (rank - r) * rows + lax.broadcasted_iota(jnp.int32, (rows, rows), 0)
        query_at = rank * rows + lax.broadcasted_iota(jnp.int32, (rows, rows), 1)
        allowed = (key_at <= query_at) & (key_at >= begin_ref[...])
        bias[r * rows : (r + 1) * rows, :] = jnp.where(allowed, 0.0, NEG_LARGE)

    def one_group(group, carry):
        query = queries[group]
        total = jnp.zeros((1, GROUP * rows), F32)
        mixed = jnp.zeros((HEAD_WIDTH, GROUP * rows), F32)
        for r in range(ranks):
            at = slice(r * rows, (r + 1) * rows)
            scores = lax.dot_general(
                keys[group, at, :], query, across, preferred_element_type=F32
            )
            weight = jnp.exp(scores + jnp.concatenate([bias[at, :]] * GROUP, axis=1))
            total += jnp.sum(weight, axis=0, keepdims=True)
            mixed += lax.dot_general(
                values[group, at, :],
                weight.astype(BF16),
                (((0,), (0,)), ((), ())),
                preferred_element_type=F32,
            )
        turned = jnp.transpose(mixed * (1.0 / total)).astype(BF16)
        for h in range(GROUP):
            outs[group * GROUP + h] = turned[h * rows : (h + 1) * rows, :]
        log_ref[group] = jnp.log(total)
        return carry

    lax.fori_loop(0, KEY_VALUE_HEADS, one_group, 0)
    pack_heads(outs, out_ref, QUERY_HEADS, head)


def attend(place, span, begin, query, pairs):
    rows = query.shape[0]
    ranks = len(pairs)
    vmem = pl.BlockSpec(memory_space=pltpu.VMEM)
    elements = QUERY_HEADS * rows * rows * ranks
    return pl.pallas_call(
        partial(attend_kernel, ranks, span),
        in_specs=[pl.BlockSpec(memory_space=pltpu.SMEM)] + [vmem] * (2 + ranks),
        out_specs=[vmem, vmem],
        out_shape=[
            jax.ShapeDtypeStruct((rows, QUERY_WIDTH), BF16),
            jax.ShapeDtypeStruct((KEY_VALUE_HEADS, 1, GROUP * rows), F32),
        ],
        scratch_shapes=[
            pltpu.VMEM((KEY_VALUE_HEADS, GROUP * rows, HEAD_WIDTH), BF16),
            pltpu.VMEM((KEY_VALUE_HEADS, ranks * rows, HEAD_WIDTH), BF16),
            pltpu.VMEM((KEY_VALUE_HEADS, ranks * rows, HEAD_WIDTH), BF16),
            pltpu.VMEM((QUERY_HEADS, rows, HEAD_WIDTH), BF16),
            pltpu.VMEM((ranks * rows, rows), F32),
        ],
        compiler_params=pltpu.CompilerParams(vmem_limit_bytes=48 << 20),
        cost_estimate=pl.CostEstimate(
            flops=16 * elements * HEAD_WIDTH,
            bytes_accessed=4 * rows * QUERY_WIDTH + 2 * ranks * rows * PAIR_WIDTH,
            transcendentals=elements,
        ),
    )(place, begin[None, :], query, *pairs)


def attend_back_kernel(
    ranks, span, place_ref, begin_ref, query_ref, out_ref, grad_ref, log_ref, *refs
):
    pairs, grad_query_ref, grad_pair_ref = refs[:ranks], refs[ranks], refs[ranks + 1]
    queries, keys, values, grads, grad_queries, grad_keys, grad_values, bias, inners = refs[
        ranks + 2 :
    ]
    rows = query_ref.shape[0]
    rank, device = place_ref[0], place_ref[1]
    head = lambda h: head_at(h, span, device)
    across = (((1,), (1,)), ((), ()))
    stack_heads(query_ref, queries, jnp.asarray(SCALE, BF16))
    stack_heads(grad_ref, grads, head=head)
    for r in range(ranks):
        unpack_heads(pairs[r], keys, KEY_VALUE_HEADS, 0, r * rows)
        unpack_heads(pairs[r], values, KEY_VALUE_HEADS, KEY_WIDTH, r * rows)
        key_at = (rank - r) * rows + lax.broadcasted_iota(jnp.int32, (rows, rows), 0)
        query_at = rank * rows + lax.broadcasted_iota(jnp.int32, (rows, rows), 1)
        allowed = (key_at <= query_at) & (key_at >= begin_ref[...])
        bias[r * rows : (r + 1) * rows, :] = jnp.where(allowed, 0.0, NEG_LARGE)
    product = grad_ref[...].astype(F32) * out_ref[...].astype(F32)
    shape = (32, QUERY_WIDTH)
    mine = lane_index(shape) // HEAD_WIDTH == lax.broadcasted_iota(jnp.int32, shape, 0)
    inner = lax.dot_general(
        jnp.where(mine, 1.0, 0.0),
        product,
        across,
        precision=lax.Precision.HIGHEST,
        preferred_element_type=F32,
    )
    for h in range(QUERY_HEADS):
        at = pl.multiple_of((head(h) % GROUP) * rows, rows)
        inners[head(h) // GROUP, :, pl.ds(at, rows)] = inner[h : h + 1, :]

    def one_group(group, carry):
        query, grad = queries[group], grads[group]
        log_total, inner = log_ref[group], inners[group]
        total = jnp.zeros((HEAD_WIDTH, GROUP * rows), F32)
        for r in range(ranks):
            at = slice(r * rows, (r + 1) * rows)
            key = keys[group, at, :]
            scores = lax.dot_general(key, query, across, preferred_element_type=F32)
            mask = jnp.concatenate([bias[at, :]] * GROUP, axis=1)
            probability = jnp.exp(scores + mask - log_total)
            grad_prob = lax.dot_general(
                values[group, at, :], grad, across, preferred_element_type=F32
            )
            grad_score = (probability * (grad_prob - inner)).astype(BF16)
            grad_keys[group, at, :] = jnp.dot(grad_score, query, preferred_element_type=F32)
            grad_values[group, at, :] = jnp.dot(
                probability.astype(BF16), grad, preferred_element_type=F32
            )
            total += lax.dot_general(
                key, grad_score, (((0,), (0,)), ((), ())), preferred_element_type=F32
            )
        turned = (jnp.transpose(total) * SCALE).astype(BF16)
        for h in range(GROUP):
            grad_queries[group * GROUP + h] = turned[h * rows : (h + 1) * rows, :]
        return carry

    lax.fori_loop(0, KEY_VALUE_HEADS, one_group, 0)
    pack_heads(grad_queries, grad_query_ref, QUERY_HEADS)
    for r in range(ranks):
        for source, offset in ((grad_keys, 0), (grad_values, KEY_WIDTH)):
            for g in range(0, KEY_VALUE_HEADS, 2):
                at = offset + g * HEAD_WIDTH
                grad_pair_ref[r, :, at : at + 2 * HEAD_WIDTH] = jnp.concatenate(
                    [
                        source[g, r * rows : (r + 1) * rows, :],
                        source[g + 1, r * rows : (r + 1) * rows, :],
                    ],
                    axis=-1,
                ).astype(BF16)


def attend_back(place, span, begin, query, out, grad, log_total, pairs):
    rows = query.shape[0]
    ranks = len(pairs)
    vmem = pl.BlockSpec(memory_space=pltpu.VMEM)
    elements = QUERY_HEADS * rows * rows * ranks
    heads = pltpu.VMEM((QUERY_HEADS, rows, HEAD_WIDTH), BF16)
    one_row = pltpu.VMEM((KEY_VALUE_HEADS, 1, GROUP * rows), F32)
    stacked = pltpu.VMEM((KEY_VALUE_HEADS, GROUP * rows, HEAD_WIDTH), BF16)
    return pl.pallas_call(
        partial(attend_back_kernel, ranks, span),
        in_specs=[pl.BlockSpec(memory_space=pltpu.SMEM)] + [vmem] * (5 + ranks),
        out_specs=[vmem, vmem],
        out_shape=[
            jax.ShapeDtypeStruct((rows, QUERY_WIDTH), BF16),
            jax.ShapeDtypeStruct((ranks, rows, PAIR_WIDTH), BF16),
        ],
        scratch_shapes=[
            stacked,
            pltpu.VMEM((KEY_VALUE_HEADS, ranks * rows, HEAD_WIDTH), BF16),
            pltpu.VMEM((KEY_VALUE_HEADS, ranks * rows, HEAD_WIDTH), BF16),
            stacked,
            heads,
            pltpu.VMEM((KEY_VALUE_HEADS, ranks * rows, HEAD_WIDTH), F32),
            pltpu.VMEM((KEY_VALUE_HEADS, ranks * rows, HEAD_WIDTH), F32),
            pltpu.VMEM((ranks * rows, rows), F32),
            one_row,
        ],
        compiler_params=pltpu.CompilerParams(vmem_limit_bytes=56 << 20),
        cost_estimate=pl.CostEstimate(
            flops=40 * elements * HEAD_WIDTH,
            bytes_accessed=6 * rows * QUERY_WIDTH + 6 * ranks * rows * PAIR_WIDTH,
            transcendentals=elements,
        ),
    )(place, begin[None, :], query, out, grad, log_total, *pairs)


def unposition_kernel(query_ref, pair_ref, raw_ref, cosine_ref, sine_ref, gain_ref, out_ref, sum_ref):
    column = pl.program_id(0)
    tiles = raw_ref.shape[1] // LANES

    def back(source, tile, row):
        at = slice(tile * LANES, (tile + 1) * LANES)
        grad = source[:, at].astype(F32)
        raw = raw_ref[:, at]
        scale = head_scale(raw)
        grad = grad * cosine_ref[...] - turn(grad * sine_ref[...])
        total = jnp.sum(grad * raw * scale, axis=0, keepdims=True)
        grad = grad * gain_ref[row : row + 1, :]
        grad = scale * (grad - raw * scale * scale * head_mean(grad * raw))
        out_ref[:, at] = grad.astype(BF16)
        return total

    @pl.when(column == 0)
    def _():
        sum_ref[...] = jnp.zeros_like(sum_ref)

    @pl.when(column < 2)
    def _():
        sum_ref[0:1, :] += sum(back(query_ref, tile, 0) for tile in range(tiles))

    @pl.when(column == 2)
    def _():
        sum_ref[1:2, :] += sum(back(pair_ref, tile, 1) for tile in range(tiles // 2))
        out_ref[:, KEY_WIDTH:] = pair_ref[:, KEY_WIDTH:]


def unposition(grad_query, grad_pair, raw, cosine, sine, gains):
    rows = raw.shape[0]
    block = PAIR_WIDTH
    whole = lambda j: (0, 0)
    return pl.pallas_call(
        unposition_kernel,
        grid=(PROJ_WIDTH // block,),
        in_specs=[
            pl.BlockSpec((rows, block), lambda j: (0, jnp.minimum(j, 1))),
            pl.BlockSpec((rows, block), whole),
            pl.BlockSpec((rows, block), lambda j: (0, j)),
            pl.BlockSpec((rows, LANES), whole),
            pl.BlockSpec((rows, LANES), whole),
            pl.BlockSpec((8, LANES), whole),
        ],
        out_specs=[
            pl.BlockSpec((rows, block), lambda j: (0, j)),
            pl.BlockSpec((8, LANES), whole),
        ],
        out_shape=[
            jax.ShapeDtypeStruct((rows, PROJ_WIDTH), BF16),
            jax.ShapeDtypeStruct((8, LANES), F32),
        ],
        compiler_params=pltpu.CompilerParams(vmem_limit_bytes=32 << 20),
        cost_estimate=pl.CostEstimate(
            flops=40 * rows * PROJ_WIDTH, bytes_accessed=8 * rows * PROJ_WIDTH, transcendentals=0
        ),
    )(grad_query, grad_pair, raw, cosine, sine, gains)


def tail_kernel(count, *refs):
    mixed, down_ref, out_grad_ref = refs[:count], refs[count], refs[count + 1]
    even, odd_ref, held = refs[count + 2 : -2], refs[-2], refs[-1]
    k = pl.program_id(0)
    for j in range(count):

        @pl.when(k == j)
        def _(j=j):
            held[...] = mixed[j][...]

    part = jnp.dot(held[...], down_ref[...], preferred_element_type=F32).astype(BF16)
    rows = part.shape[0]
    for j in range(count // 2):

        @pl.when(k == 2 * j)
        def _(j=j):
            even[j][:rows, :] = part
            even[j][rows:, :] = out_grad_ref[...]

    @pl.when(k % 2 == 1)
    def _():
        odd_ref[0, :rows, :] = part
        odd_ref[0, rows:, :] = out_grad_ref[...]


def tail_product(mixed, down, out_grad):
    count = len(mixed)
    rows, units = mixed[0].shape
    width = down.shape[1]
    extra = out_grad.shape[0] // count
    high = rows + extra
    whole = lambda k: (0, 0)
    *even, odd = pl.pallas_call(
        partial(tail_kernel, count),
        grid=(count,),
        in_specs=[pl.BlockSpec((rows, units), whole)] * count
        + [
            pl.BlockSpec((units, width), whole),
            pl.BlockSpec((extra, width), lambda k: (k, 0)),
        ],
        out_specs=[pl.BlockSpec((high, width), whole)] * (count // 2)
        + [pl.BlockSpec((1, high, width), lambda k: (k // 2, 0, 0))],
        out_shape=[jax.ShapeDtypeStruct((high, width), BF16)] * (count // 2)
        + [jax.ShapeDtypeStruct((count // 2, high, width), BF16)],
        scratch_shapes=[pltpu.VMEM((rows, units), BF16)],
        compiler_params=pltpu.CompilerParams(vmem_limit_bytes=48 << 20),
        cost_estimate=pl.CostEstimate(
            flops=2 * rows * count * units * width,
            bytes_accessed=2 * count * high * width,
            transcendentals=0,
        ),
    )(*mixed, down, out_grad)
    return even, odd


def inverse_rms(values):
    return lax.rsqrt(jnp.mean(values * values, axis=-1, keepdims=True) + EPSILON)


def norm_back(grad_out, values, scale):
    return scale * (
        grad_out - values * scale * scale * jnp.mean(grad_out * values, axis=-1, keepdims=True)
    )


def rope_tables(position):
    half_size = HEAD_WIDTH // 2
    inverse_freq = jnp.exp(
        jnp.arange(half_size, dtype=F32) * (-2.0 * math.log(10000.0) / HEAD_WIDTH)
    )
    angle = position.astype(F32)[:, None] * inverse_freq[None, :]
    copies = LANES // half_size
    return (jnp.tile(jnp.cos(angle), (1, copies)), jnp.tile(jnp.sin(angle), (1, copies)))


def gain_rows(gain):
    wide = jnp.tile(gain.astype(F32), LANES // HEAD_WIDTH)
    return jnp.broadcast_to(wide[None, :], (8, LANES))


def layer(
    block_input,
    doc_starts,
    attn_gain,
    query_key_value_weight,
    query_gain,
    key_gain,
    out_weight,
    mlp_gain,
    gateup_weight,
    down_weight,
    cotangent,
):
    count, rows, width = block_input.shape
    assert count == 1
    size = lax.axis_size(FSDP)
    ranks = lax.axis_size(SEQ)
    me = lax.axis_index(FSDP)
    rank = lax.axis_index(SEQ)
    depth = query_key_value_weight.shape[0]
    units = down_weight.shape[0]
    span = out_weight.shape[0] // HEAD_WIDTH if tuned() else None
    contract = (((0,), (0,)), ((), ()))
    transposed = (((1,), (1,)), ((), ()))

    place = jnp.stack([rank, me])

    qkv_pieces = gather_finish(gather_start(query_key_value_weight))
    gain_pieces = gather_small(jnp.stack([attn_gain, mlp_gain]))
    out_held = gather_start(out_weight)

    def gateup_columns(half, k):
        at = (half * size + peer(k)) * units
        return lax.dynamic_slice_in_dim(gateup_weight, at, units, axis=1)

    if tuned():
        even = rank % 2 == 0
        fetched = exchange([gateup_columns(rank % 2, k) for k in range(size)])
        mine = collect_rows(place, fetched)
        other = seq_move(mine, [(0, 1), (1, 0), (2, 3), (3, 2)])
        gateup_mine = jnp.concatenate(
            [jnp.where(even, mine, other), jnp.where(even, other, mine)], axis=1
        )
    else:
        gateup_mine = rows_to_absolute(
            exchange(
                [
                    jnp.concatenate([gateup_columns(0, k), gateup_columns(1, k)], axis=1)
                    for k in range(size)
                ],
            )
        )
    grad_low = cotangent.reshape(rows, width)
    grad_held = gather_start(grad_low)

    position = rank * rows + jnp.arange(rows, dtype=jnp.int32)
    starts = doc_starts.reshape(-1)
    begin = jnp.max(
        jnp.where(starts[None, :] <= position[:, None], starts[None, :], 0), axis=-1
    )
    cosine, sine = rope_tables(position - begin)
    query_gains, key_gains = gain_rows(query_gain), gain_rows(key_gain)

    tokens_in = block_input.reshape(rows, width)
    inputs = tokens_in.astype(F32)
    scale_attn = inverse_rms(inputs)
    order = peer(jnp.arange(size))
    gain_attn = gain_pieces[:, 0][order].reshape(width).astype(F32)
    gain_mlp = gain_pieces[:, 1][order].reshape(width).astype(F32)
    normed_low = (inputs * scale_attn * gain_attn).astype(BF16)
    mix_gains = jnp.concatenate([query_gains[:1], key_gains[:1], query_gains[:6]], axis=0)
    raw, query, pair, split = project(place, normed_low, cosine, sine, mix_gains, qkv_pieces, depth)
    pairs = [pair]
    for d in range(1, ranks):
        pairs.append(seq_move(pair, [(j, j + d) for j in range(ranks - d)]))
    out_pieces = gather_finish(out_held, pair)
    attn_tok, log_total = attend(place, span, begin, query, pairs)
    hidden, mlp_low = add_heads(attn_tok, tokens_in, gain_mlp, out_pieces)

    mlp_held = gather_start(mlp_low)
    mixed, grads_gu, parts = [], [], []
    grad_pieces = joined(gather_finish(grad_held, mlp_low))
    mlp_pieces = list(mlp_held[:2]) if tuned() else joined(gather_finish(mlp_held))
    for k in range(size):
        if tuned() and k == 2:
            mlp_pieces += joined(gather_finish(mlp_held, parts[1])[2:])
        if k:
            (mlp_pieces[k],) = after((mlp_pieces[k],), parts[k - 1])
        grad_here = lax.optimization_barrier(
            lax.dot_general(
                grad_pieces[k], down_weight, transposed, preferred_element_type=F32
            )
        )
        gate_up = jnp.dot(mlp_pieces[k], gateup_mine, preferred_element_type=F32)
        gate = gate_up[:, :units]
        upper = gate_up[:, units:]
        sigmoid_gate = jax.nn.sigmoid(gate)
        activated = gate * sigmoid_gate
        mixed.append((activated * upper).astype(BF16))
        grad_gate = grad_here * upper * sigmoid_gate * (1.0 + gate * (1.0 - sigmoid_gate))
        grad_upper = grad_here * activated
        grads_gu.append(jnp.concatenate([grad_gate, grad_upper], axis=-1).astype(BF16))
        parts.append(
            lax.dot_general(
                grads_gu[k], gateup_mine, transposed, preferred_element_type=F32
            ).astype(BF16)
        )
    grad_mlp_in = scatter_sum(parts)

    if tuned():
        down_cuts = down_product(mixed, grad_pieces, 2)
        gateup_parts = gateup_product(place, mlp_pieces, grads_gu, depth, 0, 2)
        gateup_parts += gateup_product(place, mlp_pieces, grads_gu, depth, 2, 2)
    else:
        mixed_low = jnp.concatenate(mixed, axis=0)
        down_cuts = [
            lax.dot_general(
                mixed_low,
                jnp.concatenate(grad_pieces, axis=0),
                contract,
                preferred_element_type=F32,
            ).astype(BF16)
        ]
        grad_gateup = lax.dot_general(
            jnp.concatenate(mlp_pieces, axis=0),
            jnp.concatenate(grads_gu, axis=0),
            contract,
            preferred_element_type=F32,
        ).astype(BF16)
        gateup_parts = [grad_gateup[k * depth : (k + 1) * depth] for k in range(size)]
    total_down = jnp.concatenate([seq_sum(cut) for cut in down_cuts], axis=1).astype(F32)
    if tuned():
        total_gateup = summed = None
        for p in reversed(range(len(gateup_parts))):
            part = gateup_parts[p]
            summed = seq_sum(part, summed)
            for k in (2 * p, 2 * p + 1):
                piece = lax.dynamic_slice_in_dim(summed, (peer(k) % 2) * depth, depth, axis=0)
                piece = swap(piece, k) if k else piece
                total_gateup = put_columns(place, total_gateup, piece, k, units, size)
    else:
        total_gateup = jnp.zeros((depth, 2 * units * size), F32)
        for k, part in enumerate(exchange(gateup_parts)):
            summed = seq_sum(part).astype(F32)
            for half in range(2):
                total_gateup = lax.dynamic_update_slice(
                    total_gateup,
                    summed[:, half * units : (half + 1) * units],
                    (0, (half * size + k) * units),
                )

    (hidden,) = after((hidden,), parts[0])
    scale_mlp = inverse_rms(hidden)
    grad_hidden = grad_low.astype(F32) + norm_back(
        grad_mlp_in * gain_mlp, hidden, scale_mlp
    )
    grad_mlp_gain = jnp.sum(grad_mlp_in * hidden * scale_mlp, axis=0)
    grad_hidden_low = grad_hidden.astype(BF16)

    out_all = jnp.concatenate(
        after([part for entry in out_pieces for part in entry], parts[2]), axis=0
    )
    grad_attn_low = lax.dot_general(
        grad_hidden_low, out_all, transposed, preferred_element_type=F32
    ).astype(BF16)
    grad_query, grad_pairs = attend_back(
        place, span, begin, query, attn_tok, grad_attn_low, log_total, pairs
    )
    back_pairs = [(j + 1, j) for j in range(ranks - 1)]
    carry = grad_pairs[ranks - 1]
    for r in range(ranks - 2, -1, -1):
        carry = add_low(grad_pairs[r], seq_move(carry, back_pairs))
    grad_proj, gain_sums = unposition(grad_query, carry, raw, cosine, sine, mix_gains)
    columns = exchange_tokens(split)
    entries = gather_direct(grad_proj)
    grad_weight = joint_product(columns, entries)
    total_qkv = seq_sum(grad_weight).astype(F32)

    late_tok, late_low = after((attn_tok, grad_hidden_low), grad_query)
    grad_out = lax.dot_general(
        late_tok, late_low, contract, preferred_element_type=F32
    ).astype(BF16)
    held = out_weight.shape[0]
    if tuned():
        late_mixed = after(mixed, grad_query)
        even, odd = tail_product(late_mixed, down_weight, grad_out)
        sums = scatter_direct(even, odd)
        out_sum, shard_out = sums[:rows], sums[rows:]
    else:
        shard_out = scatter_sum([grad_out[k * held : (k + 1) * held] for k in range(size)])
        out_sum = scatter_sum(
            [jnp.dot(m, down_weight, preferred_element_type=F32).astype(BF16) for m in mixed]
        )
    total_out = seq_sum(shard_out.astype(BF16)).astype(F32)
    (late_hidden,) = after((hidden,), grad_query)
    block_output = (late_hidden + out_sum).astype(BF16).reshape(block_input.shape)

    grad_attn_in = unproject(place, grad_proj, qkv_pieces, depth)
    grad_attn_gain = jnp.sum(grad_attn_in * (inputs * scale_attn), axis=0)
    input_grad = grad_hidden + norm_back(grad_attn_in * gain_attn, inputs, scale_attn)

    small = jnp.concatenate([grad_attn_gain, grad_mlp_gain, gain_sums[0], gain_sums[1]])
    small = sum_small(small)
    total_attn_gain = lax.dynamic_slice_in_dim(small, me * depth, depth)
    total_mlp_gain = lax.dynamic_slice_in_dim(small, width + me * depth, depth)
    heads = small[2 * width :].reshape(2, LANES // HEAD_WIDTH, HEAD_WIDTH).sum(axis=1)
    return (
        block_output,
        input_grad.reshape(block_input.shape),
        total_attn_gain,
        total_qkv,
        heads[0],
        heads[1],
        total_out,
        total_mlp_gain,
        total_gateup,
        total_down,
    )


def solution(mesh):
    return jax.shard_map(
        layer,
        mesh=mesh,
        in_specs=(
            P(FSDP, SEQ, None),
            P(FSDP, None),
            P(FSDP),
            P(FSDP, None),
            P(),
            P(),
            P(FSDP, None),
            P(FSDP),
            P(FSDP, None),
            P(FSDP, None),
            P(FSDP, SEQ, None),
        ),
        out_specs=(
            P(FSDP, SEQ, None),
            P(FSDP, SEQ, None),
            P(FSDP),
            P(FSDP, None),
            P(),
            P(),
            P(FSDP, None),
            P(FSDP),
            P(FSDP, None),
            P(FSDP, None),
        ),
        check_vma=False,
    )
```
